512 devices in a mesh: rep: 16 (over z_hi, y), shard: 32 (over x, z_lo, core).
Axes of the slice: x: 4, y: 4, z: 16 (z_hi: 4, z_lo: 4; z = z_hi * 4 + z_lo), core: 2. Of those that a mesh axis runs over, the one named last changes fastest.
Arguments:
- queries: bfloat16 [16, 4096, 256], P('rep', 'shard'), may hold values from -64 to 64
- targets: int32 [16, 4096], P('rep', 'shard'), may hold values from 0 to 16383, as said below
- samp_ids: int32 [16, 128], P('rep', 'shard'), may hold values from 0 to 5, as said below
- counts: int32 [16, 32], P('rep', 'shard'), may hold values from 1 to 4, as said below
- logq: float32 [16, 128], P('rep', 'shard'), may hold values from -9 to -5
- table: float32 [24576, 256], P('shard'), may hold values from -1 to 1
- first_moment: float32 [24576, 256], P('shard'), may hold values from -2 to 2
- second_moment: float32 [24576, 256], P('shard'), may hold values from 0.01 to 1
Outputs:
- loss: float32 [16, 4096], P('rep', 'shard')
- query_grad: float32 [16, 4096, 256], P('rep', 'shard')
- new_table: float32 [24576, 256], P('shard')
- new_first: float32 [24576, 256], P('shard')
- new_second: float32 [24576, 256], P('shard')
The draws below stay inside these ranges and needn't reach their ends.
Inputs may be any that keep to these rules, and one draw needn't show every extreme that they name: In each group some device counts 4; when a device counts 4, the device of its group whose shard index differs in the lowest bit counts at most 2. `samp_ids`: the 4 numbers listed for one device are distinct. `targets`: the slot always lies in a live block of the query's group.
All inputs are finite; a program needn't handle non-finite values.
Results may differ from the reference program's by a relative error of at most 0.0085.
Values may be sent and summed in bfloat16 or wider, within the bound.
No kernel may reach another device: no remote copies, remote signals or barrier semaphores. Data moves between devices by JAX's collectives and lax.ppermute only.
A program may use at most 64 MiB of HBM per device.

```python
import math
import jax
import jax.numpy as jnp
from jax import lax

D = 256
BLOCK = 128
BLK_DEV = 6
SAMP_DEV = 4
QUERIES = 4096
SLOTS = 128
ITEMS = 24576
N_REP = 16
N_SHARD = 32


def full_device():
    return (N_SHARD - 1 - jnp.arange(N_REP, dtype=jnp.int32) % N_SHARD).astype(jnp.int32)


def sample_plan(key):
    base = jax.random.fold_in(key, 7001)
    high_key, low_key, flip_key, order_key = jax.random.split(base, 4)
    pair_count = N_SHARD // 2
    high = jax.random.randint(high_key, (N_REP, pair_count), 1, SAMP_DEV + 1)
    low = jax.random.randint(low_key, (N_REP, pair_count), 1, SAMP_DEV - 1)
    flip = jax.random.randint(flip_key, (N_REP, pair_count), 0, 2)
    full_dev = full_device()
    full_pair = jnp.arange(pair_count, dtype=jnp.int32)[None, :] == (full_dev // 2)[:, None]
    high = jnp.where(full_pair, SAMP_DEV, high)
    flip = jnp.where(full_pair, (full_dev % 2)[:, None], flip)
    even_count = jnp.where(flip == 0, high, low)
    odd_count = jnp.where(flip == 0, low, high)
    block_counts = jnp.stack([even_count, odd_count], axis=-1).reshape(N_REP, N_SHARD).astype(jnp.int32)
    raw = jax.random.randint(order_key, (N_REP, N_SHARD, BLK_DEV), 0, 1 << 20)
    ranked = raw * BLK_DEV + jnp.arange(BLK_DEV, dtype=jnp.int32)
    order = jnp.argsort(ranked, axis=-1, stable=True)[..., :SAMP_DEV]
    return (block_counts, order.reshape(N_REP, SLOTS).astype(jnp.int32))


def table_values(key):
    return jax.random.normal(jax.random.fold_in(key, 7003), (ITEMS, D), jnp.float32) / math.sqrt(D)


def draw_table(key, part):
    return jnp.clip(table_values(key), -1.0, 1.0)


def draw_counts(key, part):
    return sample_plan(key)[0]


def draw_samp_ids(key, part):
    return sample_plan(key)[1]


def draw_targets(key, part):
    block_counts, order = sample_plan(key)
    first_key, second_key, third_key = jax.random.split(jax.random.fold_in(key, 7002), 3)
    owner = jax.random.randint(first_key, (N_REP, QUERIES), 0, N_SHARD)
    raw = jax.random.randint(second_key, (N_REP, QUERIES), 0, 1 << 16)
    own_count = jnp.take_along_axis(block_counts, owner, axis=1)
    block = raw % own_count
    item = jax.random.randint(third_key, (N_REP, QUERIES), 0, BLOCK)
    picked = (owner * (SAMP_DEV * BLOCK) + block * BLOCK + item).astype(jnp.int32)
    picked = picked.at[0, 0].set(SLOTS * BLOCK - 1)
    picked = picked.at[0, 1].set(0)
    return picked.astype(jnp.int32)


def draw_queries(key, part):
    values = jax.random.normal(jax.random.fold_in(key, 7004), (N_REP, QUERIES, D), jnp.float32)
    return jnp.clip(values, -64.0, 64.0).astype(jnp.bfloat16)


def block_scale(key, dims, cuts, least, high):
    gain = 1.0
    for dim, shards_of in cuts:
        heights = jax.random.uniform(jax.random.fold_in(jax.random.fold_in(key, 6), dim), (shards_of,), jnp.float32, least / len(cuts), high / len(cuts))
        gain = gain * jnp.repeat(jnp.exp(heights), dims[dim] // shards_of).reshape((-1,) + (1,) * (len(dims) - 1 - dim))
    return gain


def scatter_about(rng, extent, spread, most, cuts=(), held_as=jnp.bfloat16):
    entries = jax.random.normal(rng, extent, jnp.float32) * spread
    if len(cuts) > 0:
        entries = block_scale(rng, extent, cuts, -0.22, 0.18) * entries
    return jnp.clip(entries, min=-most, max=most).astype(held_as)


def setup_inputs(seed: int = 0) -> dict:
    key_list = jax.random.split(jax.random.key(seed), 9)
    return {
        "queries": draw_queries(jax.random.fold_in(key_list[8], 71), 0),
        "targets": draw_targets(jax.random.fold_in(key_list[8], 71), 0),
        "samp_ids": draw_samp_ids(jax.random.fold_in(key_list[8], 71), 0),
        "counts": draw_counts(jax.random.fold_in(key_list[8], 71), 0),
        "logq": jnp.clip(-9.0 + 4.0 * jax.random.uniform(key_list[4], (N_REP, SLOTS), jnp.float32) ** block_scale(key_list[4], (N_REP, SLOTS), ((0, 16), (1, 32)), -0.2, 0.2), -9.0, -5.0),
        "table": draw_table(jax.random.fold_in(key_list[8], 71), 0),
        "first_moment": scatter_about(key_list[6], (ITEMS, D), 0.3, 2.0, ((0, 32),), jnp.float32),
        "second_moment": jnp.clip(jnp.exp(math.log(1.0) - 4.6051702 * jax.random.uniform(key_list[7], (ITEMS, D), jnp.float32) ** block_scale(key_list[7], (ITEMS, D), ((0, 32),), -0.2, 0.2)), 0.01, 1.0),
    }


logit_scale = 2.0
beta_first = 0.9
beta_second = 0.99
learn_rate = 0.01
adam_eps = 1e-08
bias_first = 1.0 - 0.9 ** 10
bias_second = 1.0 - 0.99 ** 10
floor_value = -1e+30

def candidate_rows(group_ids):
    owner = jnp.arange(SLOTS, dtype=jnp.int32) // SAMP_DEV
    start = owner * (BLK_DEV * BLOCK) + group_ids.astype(jnp.int32) * BLOCK
    rows = start[:, None] + jnp.arange(BLOCK, dtype=jnp.int32)[None, :]
    return rows.reshape(-1)

def group_terms(table_half, group_queries, group_targets, group_ids, group_counts, group_logq):
    rows = candidate_rows(group_ids)
    items = table_half[rows]
    slot_live = jnp.arange(SLOTS, dtype=jnp.int32) % SAMP_DEV < jnp.repeat(group_counts, SAMP_DEV)
    live = jnp.repeat(slot_live, BLOCK)
    shift = jnp.repeat(group_logq, BLOCK)
    scores = logit_scale * jnp.dot(group_queries, items.T, preferred_element_type=jnp.float32) - shift[None, :]
    masked = jnp.where(live[None, :], scores, floor_value)
    top = lax.optimization_barrier(jnp.max(masked, axis=1))
    sums = lax.optimization_barrier(jnp.sum(jnp.where(live[None, :], jnp.exp(masked - top[:, None]), 0.0), axis=1))
    norm_total = top + jnp.log(sums)
    chosen = jnp.take_along_axis(scores, group_targets[:, None].astype(jnp.int32), axis=1)[:, 0]
    loss = norm_total - chosen
    onehot = (jnp.arange(SLOTS * BLOCK, dtype=jnp.int32)[None, :] == group_targets[:, None]).astype(jnp.float32)
    probs = jnp.where(live[None, :], jnp.exp(masked - norm_total[:, None]), 0.0)
    dlogit = (probs - onehot).astype(jnp.bfloat16)
    item_part = logit_scale * jnp.dot(dlogit.T, group_queries, preferred_element_type=jnp.float32)
    query_grad = logit_scale * jnp.dot(dlogit, items, preferred_element_type=jnp.float32)
    dense = jnp.zeros((ITEMS, D), jnp.float32).at[rows].add(item_part)
    return (loss, query_grad, dense)

def reference(queries, targets, samp_ids, counts, logq, table, first_moment, second_moment):
    table_half = table.astype(jnp.bfloat16)

    def one_group(carry, inputs):
        group_queries, group_targets, group_ids, group_counts, group_logq = inputs
        loss, query_grad, dense = group_terms(table_half, group_queries, group_targets, group_ids, group_counts, group_logq)
        return (carry + dense, (loss, query_grad))
    item_grad, outputs = lax.scan(one_group, jnp.zeros((ITEMS, D), jnp.float32), (queries, targets, samp_ids, counts, logq))
    loss, query_grad = outputs
    new_first = beta_first * first_moment + (1.0 - beta_first) * item_grad
    new_second = beta_second * second_moment + (1.0 - beta_second) * item_grad * item_grad
    new_table = table - learn_rate * (new_first / bias_first) / (jnp.sqrt(new_second / bias_second) + adam_eps)
    return (loss, query_grad, new_table, new_first, new_second)
```

```python
import jax
import jax.numpy as jnp
from jax import lax
from jax.experimental import pallas as pl
from jax.experimental.pallas import tpu as pltpu
from jax.sharding import Mesh, PartitionSpec as P

BLOCK = 128
D = 256
SLOTS_DEV = 4
BLOCKS_DEV = 6
NX = 4
NY = 4
NZ = 4
NC = 2
NQ = NZ * NC
SLOTS = NX * SLOTS_DEV
PART = BLOCK // NY
META = 16
CHUNK = 256
CHUNKS = NQ * BLOCK // CHUNK
QROWS = ("c", "zl")

logit_scale = 2.0
beta_first = 0.9
beta_second = 0.99
learn_rate = 0.01
adam_eps = 1e-08
bias_first = 1.0 - 0.9**10
bias_second = 1.0 - 0.99**10
floor_value = -1e30

f32 = jnp.float32
bf16 = jnp.bfloat16
i32 = jnp.int32


def vmem():
    return pl.BlockSpec(memory_space=pltpu.VMEM)


def smem():
    return pl.BlockSpec(memory_space=pltpu.SMEM)


def pack_kernel(ids, count, logq, table, queries, targets, item_out, query_out, rows, sems):
    copies = []
    for j in range(SLOTS_DEV):
        start = pl.multiple_of(ids[0, j] * BLOCK, BLOCK)
        copy = pltpu.make_async_copy(table.at[pl.ds(start, BLOCK), :], rows.at[j], sems.at[j])
        copy.start()
        copies.append(copy)
    row = lax.broadcasted_iota(i32, (META, D), 0)
    lane = lax.broadcasted_iota(i32, (META, D), 1)
    meta = jnp.where(row == 4, count[0, 0].astype(f32), 0.0)
    for j in range(SLOTS_DEV):
        whole = jnp.full((META, D), logq[0, j], f32)
        high = whole.astype(bf16).astype(f32)
        mid = (whole - high).astype(bf16).astype(f32)
        low = whole - high - mid
        ident = jnp.full((META, D), ids[0, j].astype(f32), f32)
        value = jnp.where(row == 0, high, jnp.where(row == 1, mid, jnp.where(row == 2, low, ident)))
        meta = jnp.where((lane == j) & (row < 4), value, meta)
    item_out[pl.ds(SLOTS_DEV * BLOCK, META), :] = meta.astype(bf16)
    slot = (targets[...] >> 7).astype(f32)
    item = (targets[...] & (BLOCK - 1)).astype(f32)
    both = jnp.concatenate([slot, item], axis=1)
    query_out[pl.ds(0, BLOCK), :] = queries[0]
    query_out[pl.ds(BLOCK, META), :] = jnp.broadcast_to(both, (META, D)).astype(bf16)
    for j in range(SLOTS_DEV):
        copies[j].wait()
        item_out[pl.ds(j * BLOCK, BLOCK), :] = rows[j].astype(bf16)


def slot_tables(items, live, shifts):
    lane = lax.broadcasted_iota(i32, (1, D), 1)
    number = jnp.int32(0)
    for x in range(NX):
        meta = items[x, pl.ds(SLOTS_DEV * BLOCK, META), :].astype(f32)
        row = meta[0:1] + meta[1:2] + meta[2:3]
        count = jnp.max(meta[4:5]).astype(i32)
        for j in range(SLOTS_DEV):
            shifts[x * SLOTS_DEV + j] = jnp.sum(jnp.where(lane == j, row, 0.0))
            live[number] = x * SLOTS_DEV + j
            number = number + (j < count).astype(i32)
    return number


def query_chunk(queries, b):
    return jnp.concatenate([queries[2 * b, pl.ds(0, BLOCK), :], queries[2 * b + 1, pl.ds(0, BLOCK), :]], axis=0)


def target_chunk(queries, b):
    first = queries[2 * b, pl.ds(BLOCK, META), :].astype(f32)[0:1]
    second = queries[2 * b + 1, pl.ds(BLOCK, META), :].astype(f32)[0:1]
    slot = jnp.concatenate([first[:, :BLOCK], second[:, :BLOCK]], axis=1)
    item = jnp.concatenate([first[:, BLOCK:], second[:, BLOCK:]], axis=1)
    return slot.astype(i32), item.astype(i32)


def slot_rows(items, slot):
    x = slot // SLOTS_DEV
    j = slot % SLOTS_DEV
    return items[x, pl.ds(pl.multiple_of(j * BLOCK, BLOCK), BLOCK), :]


def group_slot(place, slot):
    x = slot // SLOTS_DEV
    return x * (NQ * SLOTS_DEV) + place * SLOTS_DEV + slot % SLOTS_DEV


def products(rows, query_rows):
    return lax.dot_general(rows, query_rows, (((1,), (1,)), ((), ())), preferred_element_type=f32)


def totals_kernel(place, items, queries, out, live, shifts, tops, sums, picks):
    number = slot_tables(items, live, shifts)
    tops[...] = jnp.full(tops.shape, floor_value, f32)
    sums[...] = jnp.zeros(sums.shape, f32)
    picks[...] = jnp.zeros(picks.shape, f32)
    item_index = lax.broadcasted_iota(i32, (BLOCK, CHUNK), 0)

    def one_slot(i, carry):
        slot = live[i]
        shift = shifts[slot]
        rows = slot_rows(items, slot)
        mine = group_slot(place[0], slot)
        for b in range(CHUNKS):
            cols = pl.ds(b * CHUNK, CHUNK)
            target_slot, target_item = target_chunk(queries, b)
            wanted = jnp.where(target_slot == mine, target_item, -1)
            scores = logit_scale * products(rows, query_chunk(queries, b)) - shift
            split = scores.reshape(BLOCK // 8, 8, CHUNK)
            old = tops[:, cols]
            top = jnp.maximum(old, jnp.max(split, axis=0))
            fresh = jnp.sum(jnp.exp(split - top[None]), axis=0)
            sums[:, cols] = sums[:, cols] * jnp.exp(old - top) + fresh
            tops[:, cols] = top
            marked = jnp.where(item_index == wanted, scores, 0.0).reshape(BLOCK // 8, 8, CHUNK)
            picks[:, cols] = picks[:, cols] + jnp.sum(marked, axis=0)
        return carry

    lax.fori_loop(0, number, one_slot, 0)
    top = jnp.max(tops[...], axis=0, keepdims=True)
    total = jnp.sum(sums[...] * jnp.exp(tops[...] - top), axis=0, keepdims=True)
    norm = top + jnp.log(total)
    pick = jnp.sum(picks[...], axis=0, keepdims=True)
    norms = jnp.concatenate([norm[:, r * BLOCK : (r + 1) * BLOCK] for r in range(NQ)], axis=0)
    for d in range(NQ):
        out[d, pl.ds(0, NQ), :] = norms
        out[d, pl.ds(NQ, NQ), :] = jnp.broadcast_to(pick[:, d * BLOCK : (d + 1) * BLOCK], (NQ, BLOCK))


def grads_kernel(place, items, queries, stats, loss_out, item_out, query_out, live, shifts, gone, rows_all):
    number = slot_tables(items, live, shifts)
    item_out[...] = jnp.zeros(item_out.shape, bf16)
    for x in range(NX):
        meta = items[x, pl.ds(SLOTS_DEV * BLOCK, META), :]
        for y in range(NY):
            item_out[y * NX + x, pl.ds(SLOTS_DEV * PART, META), :] = meta
    top = stats[0, pl.ds(0, NQ), :]
    pick = stats[0, pl.ds(NQ, NQ), :]
    for r in range(1, NQ):
        top = jnp.maximum(top, stats[r, pl.ds(0, NQ), :])
        pick = pick + stats[r, pl.ds(NQ, NQ), :]
    total = jnp.zeros_like(top)
    for r in range(NQ):
        total = total + jnp.exp(stats[r, pl.ds(0, NQ), :] - top)
    norms = top + jnp.log(total)
    own = lax.broadcasted_iota(i32, norms.shape, 0) == place[1]
    loss_out[...] = jnp.sum(jnp.where(own, norms - pick, 0.0), axis=0, keepdims=True)
    item_index = lax.broadcasted_iota(i32, (BLOCK, CHUNK), 0)

    def one_slot(i, carry):
        slot = live[i]
        shift = shifts[slot]
        rows = slot_rows(items, slot)
        rows_all[i] = rows
        mine = group_slot(place[0], slot)
        part = jnp.zeros((BLOCK, D), f32)
        for b in range(CHUNKS):
            target_slot, target_item = target_chunk(queries, b)
            wanted = jnp.where(target_slot == mine, target_item, -1)
            norm = jnp.concatenate([norms[2 * b : 2 * b + 1], norms[2 * b + 1 : 2 * b + 2]], axis=1)
            query_rows = query_chunk(queries, b)
            scores = logit_scale * products(rows, query_rows) - shift
            probs = jnp.exp(scores - norm)
            dlogit = jnp.where(item_index == wanted, probs - 1.0, probs).astype(bf16)
            gone[i, :, pl.ds(b * CHUNK, CHUNK)] = dlogit
            part = part + jnp.dot(dlogit, query_rows, preferred_element_type=f32)
        part = (logit_scale * part).astype(bf16)
        x = slot // SLOTS_DEV
        j = slot % SLOTS_DEV
        for y in range(NY):
            item_out[y * NX + x, pl.ds(pl.multiple_of(j * PART, PART), PART), :] = part[y * PART : (y + 1) * PART]
        return carry

    lax.fori_loop(0, number, one_slot, 0)
    groups = (number + SLOTS_DEV - 1) // SLOTS_DEV

    def pad(i, carry):
        rows_all[i] = jnp.zeros((BLOCK, D), bf16)
        gone[i] = jnp.zeros((BLOCK, NQ * BLOCK), bf16)
        return carry

    lax.fori_loop(number, groups * SLOTS_DEV, pad, 0)
    for b in range(CHUNKS):

        def one_group(g, total):
            four = pl.ds(g * SLOTS_DEV, SLOTS_DEV)
            rows = rows_all[four].reshape(SLOTS_DEV * BLOCK, D)
            dlogit = gone[four, :, pl.ds(b * CHUNK, CHUNK)].reshape(SLOTS_DEV * BLOCK, CHUNK)
            return total + lax.dot_general(
                rows, dlogit, (((0,), (0,)), ((), ())), preferred_element_type=f32
            )

        total = lax.fori_loop(0, groups, one_group, jnp.zeros((D, CHUNK), f32))
        total = (logit_scale * total).astype(bf16)
        query_out[2 * b] = total[:, :BLOCK]
        query_out[2 * b + 1] = total[:, BLOCK:]


def gather_parts_kernel(parts, out, total):
    lane = lax.broadcasted_iota(i32, (1, D), 1)
    total[...] = jnp.zeros(total.shape, f32)
    for y in range(NY):
        meta = parts[y * NX, pl.ds(SLOTS_DEV * PART, META), :].astype(f32)
        for j in range(SLOTS_DEV):
            block = jnp.sum(jnp.where(lane == j, meta[3:4], 0.0)).astype(i32)
            piece = jnp.zeros((PART, D), f32)
            for x in range(NX):
                piece = piece + parts[y * NX + x, pl.ds(j * PART, PART), :].astype(f32)
            total[block] = total[block] + piece
    out[...] = total[...].astype(bf16)


def adam_kernel(gradient, table, first, second, table_out, first_out, second_out):
    grad = gradient[...].reshape(BLOCK, D)
    first_new = beta_first * first[...] + (1.0 - beta_first) * grad
    second_new = beta_second * second[...] + (1.0 - beta_second) * grad * grad
    first_out[...] = first_new
    second_out[...] = second_new
    table_out[...] = table[...] - learn_rate * (first_new / bias_first) / (
        jnp.sqrt(second_new / bias_second) + adam_eps
    )


def spread(value, axes, size):
    return lax.all_to_all(jnp.broadcast_to(value[None], (size,) + value.shape), axes, 0, 0, tiled=True)


def local(queries, targets, samp_ids, counts, logq, table, first_moment, second_moment):
    place = lax.axis_index("zl") * NC + lax.axis_index("c")
    own = lax.axis_index("c") * NZ + lax.axis_index("zl")
    where = jnp.stack([place, own]).astype(i32)
    item_rows, query_rows = pl.pallas_call(
        pack_kernel,
        out_shape=(
            jax.ShapeDtypeStruct((SLOTS_DEV * BLOCK + META, D), bf16),
            jax.ShapeDtypeStruct((BLOCK + META, D), bf16),
        ),
        in_specs=[smem(), smem(), smem(), pl.BlockSpec(memory_space=pl.ANY), vmem(), vmem()],
        out_specs=(vmem(), vmem()),
        scratch_shapes=[pltpu.VMEM((SLOTS_DEV, BLOCK, D), f32), pltpu.SemaphoreType.DMA((SLOTS_DEV,))],
        name="pack",
    )(samp_ids, counts, logq, table, queries, targets)

    every_query = spread(query_rows, "zl", NZ)
    every_query = lax.all_gather(every_query, "c", axis=0, tiled=True)
    every_item = spread(item_rows, "x", NX)

    tables = [pltpu.SMEM((SLOTS,), i32), pltpu.SMEM((SLOTS,), f32)]
    stats = pl.pallas_call(
        totals_kernel,
        out_shape=jax.ShapeDtypeStruct((NQ, 2 * NQ, BLOCK), f32),
        in_specs=[smem(), vmem(), vmem()],
        out_specs=vmem(),
        scratch_shapes=tables + [pltpu.VMEM((8, NQ * BLOCK), f32)] * 3,
        name="totals",
    )(where, every_item, every_query)
    stats = lax.all_to_all(stats, QROWS, 0, 0, tiled=True)

    loss, item_parts, query_parts = pl.pallas_call(
        grads_kernel,
        out_shape=(
            jax.ShapeDtypeStruct((1, BLOCK), f32),
            jax.ShapeDtypeStruct((NY * NX, SLOTS_DEV * PART + META, D), bf16),
            jax.ShapeDtypeStruct((NQ, D, BLOCK), bf16),
        ),
        in_specs=[smem(), vmem(), vmem(), vmem()],
        out_specs=(vmem(), vmem(), vmem()),
        scratch_shapes=tables
        + [pltpu.VMEM((SLOTS, BLOCK, NQ * BLOCK), bf16), pltpu.VMEM((SLOTS, BLOCK, D), bf16)],
        name="grads",
    )(where, every_item, every_query, stats)

    item_parts = lax.all_to_all(item_parts, ("y", "x"), 0, 0, tiled=True)
    rows_part = pl.pallas_call(
        gather_parts_kernel,
        out_shape=jax.ShapeDtypeStruct((BLOCKS_DEV, PART, D), bf16),
        in_specs=[vmem()],
        out_specs=vmem(),
        scratch_shapes=[pltpu.VMEM((BLOCKS_DEV, PART, D), f32)],
        name="gather_parts",
    )(item_parts)
    rows_part = jnp.sum(spread(rows_part, "zh", 4).astype(f32), axis=0)
    every_part = spread(rows_part, "y", NY)

    query_parts = lax.all_to_all(query_parts, QROWS, 0, 0, tiled=True)
    query_grad = jnp.sum(query_parts.astype(f32), axis=0).T

    block = pl.BlockSpec((BLOCK, D), lambda b: (b, 0))
    new_table, new_first, new_second = pl.pallas_call(
        adam_kernel,
        grid=(BLOCKS_DEV,),
        out_shape=(jax.ShapeDtypeStruct(table.shape, f32),) * 3,
        in_specs=[pl.BlockSpec((NY, None, PART, D), lambda b: (0, b, 0, 0)), block, block, block],
        out_specs=(block, block, block),
        name="adam",
    )(every_part, table, first_moment, second_moment)
    return loss, query_grad[None], new_table, new_first, new_second


def solution(mesh):
    fine = Mesh(mesh.devices.reshape(4, NY, NX, NZ, NC), ("zh", "y", "x", "zl", "c"))
    rep = ("zh", "y")
    shard = ("x", "zl", "c")
    in_specs = (
        P(rep, shard, None),
        P(rep, shard),
        P(rep, shard),
        P(rep, shard),
        P(rep, shard),
        P(shard, None),
        P(shard, None),
        P(shard, None),
    )
    out_specs = (
        P(rep, shard),
        P(rep, shard, None),
        P(shard, None),
        P(shard, None),
        P(shard, None),
    )
    return jax.shard_map(local, mesh=fine, in_specs=in_specs, out_specs=out_specs, check_vma=False)
```

```python
import jax
import jax.numpy as jnp
from jax import lax
from jax.experimental import pallas as pl
from jax.experimental.pallas import tpu as pltpu
from jax.sharding import Mesh, PartitionSpec as P

BLOCK = 128
D = 256
SLOTS_DEV = 4
BLOCKS_DEV = 6
NX = 4
NY = 4
NZ = 4
NC = 2
NQ = NZ * NC
SLOTS = NX * SLOTS_DEV
PART = BLOCK // NY
META = 16
CHUNK = 256
CHUNKS = NQ * BLOCK // CHUNK
TOGETHER = 4
QROWS = ("c", "zl")

logit_scale = 2.0
beta_first = 0.9
beta_second = 0.99
learn_rate = 0.01
adam_eps = 1e-08
bias_first = 1.0 - 0.9**10
bias_second = 1.0 - 0.99**10
floor_value = -1e30

f32 = jnp.float32
bf16 = jnp.bfloat16
i32 = jnp.int32


def vmem():
    return pl.BlockSpec(memory_space=pltpu.VMEM)


def hbm():
    return pl.BlockSpec(memory_space=pltpu.HBM)


def smem():
    return pl.BlockSpec(memory_space=pltpu.SMEM)


def limit(mib):
    return pltpu.CompilerParams(vmem_limit_bytes=mib << 20)


def pack_kernel(ids, count, logq, table, queries, targets, item_out, query_out, rows, sems):
    copies = []
    for j in range(SLOTS_DEV):
        start = pl.multiple_of(ids[0, j] * BLOCK, BLOCK)
        copy = pltpu.make_async_copy(table.at[pl.ds(start, BLOCK), :], rows.at[j], sems.at[j])
        copy.start()
        copies.append(copy)
    slot = (targets[...] >> 7).astype(f32)
    item = (targets[...] & (BLOCK - 1)).astype(f32)
    both = jnp.broadcast_to(jnp.concatenate([slot, item], axis=1), (META, D)).astype(bf16)
    for z in range(NZ):
        query_out[z, pl.ds(0, BLOCK), :] = queries[0]
        query_out[z, pl.ds(BLOCK, META), :] = both
    row = lax.broadcasted_iota(i32, (META, D), 0)
    lane = lax.broadcasted_iota(i32, (META, D), 1)
    meta = jnp.where(row == 4, count[0, 0].astype(f32), 0.0)
    for j in range(SLOTS_DEV):
        whole = jnp.full((META, D), logq[0, j], f32)
        high = whole.astype(bf16).astype(f32)
        mid = (whole - high).astype(bf16).astype(f32)
        low = whole - high - mid
        ident = jnp.full((META, D), ids[0, j].astype(f32), f32)
        value = jnp.where(row == 0, high, jnp.where(row == 1, mid, jnp.where(row == 2, low, ident)))
        meta = jnp.where((lane == j) & (row < 4), value, meta)
    item_out[pl.ds(SLOTS_DEV * BLOCK, META), :] = meta.astype(bf16)
    for j in range(SLOTS_DEV):
        copies[j].wait()
        item_out[pl.ds(j * BLOCK, BLOCK), :] = (logit_scale * rows[j].astype(bf16).astype(f32)).astype(bf16)


def list_live(place, pieces, rows_all, live, shifts):
    lane = lax.broadcasted_iota(i32, (1, D), 1)
    number = jnp.int32(0)
    for k in range(NX):
        x = (place[2] - k) & (NX - 1)
        meta = pieces[k][pl.ds(SLOTS_DEV * BLOCK, META), :].astype(f32)
        row = meta[0:1] + meta[1:2] + meta[2:3]
        count = jnp.max(meta[4:5]).astype(i32)
        for j in range(SLOTS_DEV):
            shifts[number] = jnp.sum(jnp.where(lane == j, row, 0.0))
            live[number] = x * (NQ * SLOTS_DEV) + place[0] * SLOTS_DEV + j
            rows_all[number] = pieces[k][pl.ds(j * BLOCK, BLOCK), :]
            number = number + (j < count).astype(i32)
    return number


def query_chunk(queries, b):
    return jnp.concatenate([queries[2 * b, pl.ds(0, BLOCK), :], queries[2 * b + 1, pl.ds(0, BLOCK), :]], axis=0)


def target_chunk(queries, b):
    first = queries[2 * b, pl.ds(BLOCK, META), :].astype(f32)[0:1]
    second = queries[2 * b + 1, pl.ds(BLOCK, META), :].astype(f32)[0:1]
    slot = jnp.concatenate([first[:, :BLOCK], second[:, :BLOCK]], axis=1)
    item = jnp.concatenate([first[:, BLOCK:], second[:, BLOCK:]], axis=1)
    return slot.astype(i32), item.astype(i32)


def products(rows, query_rows):
    return lax.dot_general(rows, query_rows, (((1,), (1,)), ((), ())), preferred_element_type=f32)


def totals_kernel(place, own, one, two, three, queries, out, rows_all, live, shifts, tops, sums, picks):
    number = list_live(place, (own, one, two, three), rows_all, live, shifts)
    tops[...] = jnp.full(tops.shape, floor_value, f32)
    sums[...] = jnp.zeros(sums.shape, f32)
    picks[...] = jnp.zeros(picks.shape, f32)
    item_index = lax.broadcasted_iota(i32, (BLOCK, CHUNK), 0)

    def one_slot(i, carry):
        shift = shifts[i]
        rows = rows_all[i]
        mine = live[i]
        for b in range(CHUNKS):
            cols = pl.ds(b * CHUNK, CHUNK)
            target_slot, target_item = target_chunk(queries, b)
            wanted = jnp.where(target_slot == mine, target_item, -1)
            doubled = products(rows, query_chunk(queries, b))
            split = doubled.reshape(BLOCK // 8, 8, CHUNK)
            old = tops[:, cols]
            top = jnp.maximum(old, jnp.max(split, axis=0) - shift)
            base = top + shift
            fresh = jnp.sum(jnp.exp(split - base[None]), axis=0)
            sums[:, cols] = sums[:, cols] * jnp.exp(old - top) + fresh
            tops[:, cols] = top
            marked = jnp.where(item_index == wanted, doubled - shift, 0.0).reshape(BLOCK // 8, 8, CHUNK)
            picks[:, cols] = picks[:, cols] + jnp.sum(marked, axis=0)
        return carry

    lax.fori_loop(0, number, one_slot, 0)
    top = jnp.max(tops[...], axis=0, keepdims=True)
    total = jnp.sum(sums[...] * jnp.exp(tops[...] - top), axis=0, keepdims=True)
    norm = top + jnp.log(total)
    pick = jnp.sum(picks[...], axis=0, keepdims=True)
    norms = jnp.concatenate([norm[:, r * BLOCK : (r + 1) * BLOCK] for r in range(NQ)], axis=0)
    for d in range(NQ):
        out[d, pl.ds(0, NQ), :] = norms
        out[d, pl.ds(NQ, NQ), :] = jnp.broadcast_to(pick[:, d * BLOCK : (d + 1) * BLOCK], (NQ, BLOCK))


def item_kernel(
    place, own, one, two, three, queries, stats, number_out, loss_out, item_out, gone, rows_all, live, shifts
):
    pieces = (own, one, two, three)
    number = list_live(place, pieces, rows_all, live, shifts)
    number_out[0] = number
    item_out[...] = jnp.zeros(item_out.shape, bf16)
    for k in range(NX):
        x = (place[2] - k) & (NX - 1)
        meta = pieces[k][pl.ds(SLOTS_DEV * BLOCK, META), :]
        for y in range(NY):
            item_out[y * NX + x, pl.ds(SLOTS_DEV * PART, META), :] = meta
    top = stats[0, pl.ds(0, NQ), :]
    pick = stats[0, pl.ds(NQ, NQ), :]
    for r in range(1, NQ):
        top = jnp.maximum(top, stats[r, pl.ds(0, NQ), :])
        pick = pick + stats[r, pl.ds(NQ, NQ), :]
    total = jnp.zeros_like(top)
    for r in range(NQ):
        total = total + jnp.exp(stats[r, pl.ds(0, NQ), :] - top)
    norms = top + jnp.log(total)
    mine = lax.broadcasted_iota(i32, norms.shape, 0) == place[1]
    loss_out[...] = jnp.sum(jnp.where(mine, norms - pick, 0.0), axis=0, keepdims=True)
    item_index = lax.broadcasted_iota(i32, (BLOCK, CHUNK), 0)

    def one_slot(i, carry):
        shift = shifts[i]
        rows = rows_all[i]
        slot = live[i]
        part = jnp.zeros((BLOCK, D), f32)
        for b in range(CHUNKS):
            target_slot, target_item = target_chunk(queries, b)
            wanted = jnp.where(target_slot == slot, target_item, -1)
            norm = jnp.concatenate([norms[2 * b : 2 * b + 1], norms[2 * b + 1 : 2 * b + 2]], axis=1)
            query_rows = query_chunk(queries, b)
            probs = jnp.exp(products(rows, query_rows) - (norm + shift))
            dlogit = jnp.where(item_index == wanted, probs - 1.0, probs).astype(bf16)
            gone[i, :, pl.ds(b * CHUNK, CHUNK)] = dlogit
            part = part + jnp.dot(dlogit, query_rows, preferred_element_type=f32)
        part = (logit_scale * part).astype(bf16)
        x = slot // (NQ * SLOTS_DEV)
        j = slot % SLOTS_DEV
        for y in range(NY):
            item_out[y * NX + x, pl.ds(pl.multiple_of(j * PART, PART), PART), :] = part[y * PART : (y + 1) * PART]
        return carry

    lax.fori_loop(0, number, one_slot, 0)

    def pad(i, carry):
        rows_all[i] = jnp.zeros((BLOCK, D), bf16)
        gone[i] = jnp.zeros((BLOCK, NQ * BLOCK), bf16)
        return carry

    lax.fori_loop(number, (number + TOGETHER - 1) // TOGETHER * TOGETHER, pad, 0)


def query_kernel(number, rows_all, gone, out, total):
    total[...] = jnp.zeros(total.shape, f32)

    def one_group(g, carry):
        some = pl.ds(g * TOGETHER, TOGETHER)
        rows = rows_all[some].reshape(TOGETHER * BLOCK, D).T
        for b in range(CHUNKS):
            cols = pl.ds(b * CHUNK, CHUNK)
            dlogit = gone[some, :, cols].reshape(TOGETHER * BLOCK, CHUNK)
            total[:, cols] = total[:, cols] + jnp.dot(rows, dlogit, preferred_element_type=f32)
        return carry

    lax.fori_loop(0, (number[0] + TOGETHER - 1) // TOGETHER, one_group, 0)
    for r in range(NQ):
        out[r] = total[:, pl.ds(r * BLOCK, BLOCK)].astype(bf16)


def gather_parts_kernel(parts, out, total):
    lane = lax.broadcasted_iota(i32, (1, D), 1)
    total[...] = jnp.zeros(total.shape, f32)
    for y in range(NY):
        meta = parts[y * NX, pl.ds(SLOTS_DEV * PART, META), :].astype(f32)
        for j in range(SLOTS_DEV):
            block = jnp.sum(jnp.where(lane == j, meta[3:4], 0.0)).astype(i32)
            piece = jnp.zeros((PART, D), f32)
            for x in range(NX):
                piece = piece + parts[y * NX + x, pl.ds(j * PART, PART), :].astype(f32)
            total[block] = total[block] + piece
    out[...] = total[...].astype(bf16)


def adam_kernel(gradient, table, first, second, table_out, first_out, second_out, tables, firsts, seconds, sems):
    copies = []
    for b in range(BLOCKS_DEV):
        rows = pl.ds(b * BLOCK, BLOCK)
        grad = gradient[:, b].reshape(BLOCK, D)
        first_new = beta_first * first[rows, :] + (1.0 - beta_first) * grad
        second_new = beta_second * second[rows, :] + (1.0 - beta_second) * grad * grad
        firsts[rows, :] = first_new
        seconds[rows, :] = second_new
        tables[rows, :] = table[rows, :] - learn_rate * (first_new / bias_first) / (
            jnp.sqrt(second_new / bias_second) + adam_eps
        )
        for n, (value, out) in enumerate(((tables, table_out), (firsts, first_out), (seconds, second_out))):
            copy = pltpu.make_async_copy(value.at[rows, :], out.at[rows, :], sems.at[b, n])
            copy.start()
            copies.append(copy)
    for copy in copies:
        copy.wait()


def spread(value, axes, size):
    return lax.all_to_all(jnp.broadcast_to(value[None], (size,) + value.shape), axes, 0, 0, tiled=True)


def step(queries, targets, samp_ids, counts, logq, table, first_moment, second_moment):
    place = lax.axis_index("zl") * NC + lax.axis_index("c")
    own = lax.axis_index("c") * NZ + lax.axis_index("zl")
    where = jnp.stack([place, own, lax.axis_index("x")]).astype(i32)
    item_shape = jax.ShapeDtypeStruct((SLOTS_DEV * BLOCK + META, D), bf16)
    items, query_rows = pl.pallas_call(
        pack_kernel,
        out_shape=(item_shape, jax.ShapeDtypeStruct((NZ, BLOCK + META, D), bf16)),
        in_specs=[smem(), smem(), smem(), hbm(), vmem(), vmem()],
        out_specs=(vmem(), vmem()),
        scratch_shapes=[pltpu.VMEM((SLOTS_DEV, BLOCK, D), f32), pltpu.SemaphoreType.DMA((SLOTS_DEV,))],
        name="pack",
    )(samp_ids, counts, logq, table, queries, targets)

    every_query = lax.all_to_all(query_rows, "zl", 0, 0, tiled=True)
    pieces = [items]
    for k in range(1, NX):
        pieces.append(lax.ppermute(items, "x", [(i, (i + k) % NX) for i in range(NX)]))
    every_query = lax.all_gather(every_query, "c", axis=0, tiled=True)

    tables = [pltpu.SMEM((SLOTS + 1,), i32), pltpu.SMEM((SLOTS + 1,), f32)]
    rows_spec = pltpu.VMEM((SLOTS + 1, BLOCK, D), bf16)
    stats = pl.pallas_call(
        totals_kernel,
        out_shape=jax.ShapeDtypeStruct((NQ, 2 * NQ, BLOCK), f32),
        in_specs=[smem()] + [vmem()] * (NX + 1),
        out_specs=vmem(),
        scratch_shapes=[rows_spec] + tables + [pltpu.VMEM((8, NQ * BLOCK), f32)] * 3,
        compiler_params=limit(10),
        name="totals",
    )(where, *pieces, every_query)
    stats = lax.all_to_all(stats, QROWS, 0, 0, tiled=True)

    number, loss, item_parts, gone, rows_all = pl.pallas_call(
        item_kernel,
        out_shape=(
            jax.ShapeDtypeStruct((1,), i32),
            jax.ShapeDtypeStruct((1, BLOCK), f32),
            jax.ShapeDtypeStruct((NY * NX, SLOTS_DEV * PART + META, D), bf16),
            jax.ShapeDtypeStruct((SLOTS, BLOCK, NQ * BLOCK), bf16),
            jax.ShapeDtypeStruct((SLOTS + 1, BLOCK, D), bf16),
        ),
        in_specs=[smem()] + [vmem()] * (NX + 2),
        out_specs=(smem(), vmem(), vmem(), vmem(), vmem()),
        scratch_shapes=tables,
        compiler_params=limit(16),
        name="items",
    )(where, *pieces, every_query, stats)

    item_parts = lax.all_to_all(item_parts, ("y", "x"), 0, 0, tiled=True)
    query_parts = pl.pallas_call(
        query_kernel,
        out_shape=jax.ShapeDtypeStruct((NQ, D, BLOCK), bf16),
        in_specs=[smem(), vmem(), vmem()],
        out_specs=vmem(),
        scratch_shapes=[pltpu.VMEM((D, NQ * BLOCK), f32)],
        compiler_params=limit(12),
        cost_estimate=pl.CostEstimate(flops=1 << 30, bytes_accessed=6 << 20, transcendentals=0),
        name="query_parts",
    )(number, rows_all, gone)
    part = pl.pallas_call(
        gather_parts_kernel,
        out_shape=jax.ShapeDtypeStruct((BLOCKS_DEV, PART, D), bf16),
        in_specs=[vmem()],
        out_specs=vmem(),
        scratch_shapes=[pltpu.VMEM((BLOCKS_DEV, PART, D), f32)],
        compiler_params=limit(4),
        name="gather_parts",
    )(item_parts)
    other = lax.ppermute(part, "zh", [(0, 1), (1, 0), (2, 3), (3, 2)])
    part = lax.optimization_barrier((part.astype(f32) + other.astype(f32)).astype(bf16))
    other = lax.ppermute(part, "zh", [(1, 2), (2, 1), (3, 0), (0, 3)])
    part = part.astype(f32) + other.astype(f32)
    query_parts = lax.all_to_all(query_parts, QROWS, 0, 0, tiled=True)
    query_grad = jnp.sum(query_parts.astype(f32), axis=0).T
    every_part = spread(part, "y", NY)

    new_table, new_first, new_second = pl.pallas_call(
        adam_kernel,
        out_shape=(jax.ShapeDtypeStruct(table.shape, f32),) * 3,
        in_specs=[vmem()] * 4,
        out_specs=(hbm(),) * 3,
        scratch_shapes=[pltpu.VMEM(table.shape, f32)] * 3 + [pltpu.SemaphoreType.DMA((BLOCKS_DEV, 3))],
        compiler_params=limit(12),
        name="adam",
    )(every_part, table, first_moment, second_moment)
    return loss, query_grad[None], new_table, new_first, new_second


def solution(mesh):
    fine = Mesh(mesh.devices.reshape(4, NY, NX, NZ, NC), ("zh", "y", "x", "zl", "c"))
    rep = ("zh", "y")
    shard = ("x", "zl", "c")
    in_specs = (
        P(rep, shard, None),
        P(rep, shard),
        P(rep, shard),
        P(rep, shard),
        P(rep, shard),
        P(shard, None),
        P(shard, None),
        P(shard, None),
    )
    out_specs = (
        P(rep, shard),
        P(rep, shard, None),
        P(shard, None),
        P(shard, None),
        P(shard, None),
    )
    return jax.shard_map(step, mesh=fine, in_specs=in_specs, out_specs=out_specs, check_vma=False)
```

```python
import jax
import jax.numpy as jnp
from jax import lax
from jax.experimental import pallas as pl
from jax.experimental.pallas import tpu as pltpu
from jax.sharding import Mesh, PartitionSpec as P


BLOCK = 128
D = 256
SLOTS_DEV = 4
BLOCKS_DEV = 6
NX = 4
NY = 4
NZ = 4
NC = 2
NQ = NZ * NC
SLOTS = NX * SLOTS_DEV
PART = BLOCK // NY
META = 16
CHUNK = 256
CHUNKS = NQ * BLOCK // CHUNK
TOGETHER = 4
QROWS = ("c", "zl")

logit_scale = 2.0
beta_first = 0.9
beta_second = 0.99
learn_rate = 0.01
adam_eps = 1e-08
bias_first = 1.0 - 0.9**10
bias_second = 1.0 - 0.99**10
floor_value = -1e30

f32 = jnp.float32
bf16 = jnp.bfloat16
i32 = jnp.int32


def vmem():
    return pl.BlockSpec(memory_space=pltpu.VMEM)


def hbm():
    return pl.BlockSpec(memory_space=pltpu.HBM)


def smem():
    return pl.BlockSpec(memory_space=pltpu.SMEM)


def limit(mib):
    return pltpu.CompilerParams(vmem_limit_bytes=mib << 20)


def pack_kernel(ids, count, logq, table, queries, targets, item_out, query_out, rows, sems):
    copies = []
    for j in range(SLOTS_DEV):
        start = pl.multiple_of(ids[0, j] * BLOCK, BLOCK)
        copy = pltpu.make_async_copy(table.at[pl.ds(start, BLOCK), :], rows.at[j], sems.at[j])
        copy.start()
        copies.append(copy)
    slot = (targets[...] >> 7).astype(f32)
    item = (targets[...] & (BLOCK - 1)).astype(f32)
    both = jnp.broadcast_to(jnp.concatenate([slot, item], axis=1), (META, D)).astype(bf16)
    for z in range(NZ):
        query_out[z, pl.ds(0, BLOCK), :] = queries[0]
        query_out[z, pl.ds(BLOCK, META), :] = both
    row = lax.broadcasted_iota(i32, (META, D), 0)
    lane = lax.broadcasted_iota(i32, (META, D), 1)
    meta = jnp.where(row == 4, count[0, 0].astype(f32), 0.0)
    for j in range(SLOTS_DEV):
        whole = jnp.full((META, D), logq[0, j], f32)
        high = whole.astype(bf16).astype(f32)
        mid = (whole - high).astype(bf16).astype(f32)
        low = whole - high - mid
        ident = jnp.full((META, D), ids[0, j].astype(f32), f32)
        value = jnp.where(row == 0, high, jnp.where(row == 1, mid, jnp.where(row == 2, low, ident)))
        meta = jnp.where((lane == j) & (row < 4), value, meta)
    item_out[pl.ds(SLOTS_DEV * BLOCK, META), :] = meta.astype(bf16)
    for j in range(SLOTS_DEV):
        copies[j].wait()
        item_out[pl.ds(j * BLOCK, BLOCK), :] = (logit_scale * rows[j].astype(bf16).astype(f32)).astype(bf16)


def list_live(place, pieces, rows_all, live, shifts):
    lane = lax.broadcasted_iota(i32, (1, D), 1)
    number = jnp.int32(0)
    for k in range(NX):
        x = (place[2] - k) & (NX - 1)
        meta = pieces[k][pl.ds(SLOTS_DEV * BLOCK, META), :].astype(f32)
        row = meta[0:1] + meta[1:2] + meta[2:3]
        count = jnp.max(meta[4:5]).astype(i32)
        for j in range(SLOTS_DEV):
            shifts[number] = jnp.sum(jnp.where(lane == j, row, 0.0))
            live[number] = x * (NQ * SLOTS_DEV) + place[0] * SLOTS_DEV + j
            rows_all[number] = pieces[k][pl.ds(j * BLOCK, BLOCK), :]
            number = number + (j < count).astype(i32)
    return number


def query_chunk(queries, b):
    return jnp.concatenate([queries[2 * b, pl.ds(0, BLOCK), :], queries[2 * b + 1, pl.ds(0, BLOCK), :]], axis=0)


def target_chunk(queries, b):
    first = queries[2 * b, pl.ds(BLOCK, META), :].astype(f32)[0:1]
    second = queries[2 * b + 1, pl.ds(BLOCK, META), :].astype(f32)[0:1]
    slot = jnp.concatenate([first[:, :BLOCK], second[:, :BLOCK]], axis=1)
    item = jnp.concatenate([first[:, BLOCK:], second[:, BLOCK:]], axis=1)
    return slot.astype(i32), item.astype(i32)


def products(rows, query_rows):
    return lax.dot_general(rows, query_rows, (((1,), (1,)), ((), ())), preferred_element_type=f32)


def totals_kernel(place, own, one, two, three, queries, out, rows_all, live, shifts, taken, tops, sums, picks):
    number = list_live(place, (own, one, two, three), rows_all, live, shifts)
    tops[...] = jnp.full(tops.shape, floor_value, f32)
    sums[...] = jnp.zeros(sums.shape, f32)
    picks[...] = jnp.zeros(picks.shape, f32)
    taken[...] = jnp.zeros(taken.shape, f32)
    item_index = lax.broadcasted_iota(i32, (BLOCK, CHUNK), 0)

    def one_slot(i, carry):
        shift = shifts[i]
        rows = rows_all[i]
        mine = live[i]
        for b in range(CHUNKS):
            cols = pl.ds(b * CHUNK, CHUNK)
            target_slot, target_item = target_chunk(queries, b)
            wanted = jnp.where(target_slot == mine, target_item, -1)
            doubled = products(rows, query_chunk(queries, b))
            split = doubled.reshape(BLOCK // 8, 8, CHUNK)
            old = tops[:, cols]
            top = jnp.maximum(old, jnp.max(split, axis=0) - shift)
            base = top + shift
            fresh = jnp.sum(jnp.exp(split - base[None]), axis=0)
            sums[:, cols] = sums[:, cols] * jnp.exp(old - top) + fresh
            tops[:, cols] = top
            marked = jnp.where(item_index == wanted, doubled, 0.0).reshape(BLOCK // 8, 8, CHUNK)
            picks[:, cols] = picks[:, cols] + jnp.sum(marked, axis=0)
            taken[:, cols] = taken[:, cols] + jnp.where(target_slot == mine, shift, 0.0)
        return carry

    lax.fori_loop(0, number, one_slot, 0)
    top = jnp.max(tops[...], axis=0, keepdims=True)
    total = jnp.sum(sums[...] * jnp.exp(tops[...] - top), axis=0, keepdims=True)
    norm = top + jnp.log(total)
    pick = jnp.sum(picks[...], axis=0, keepdims=True) - taken[...]
    norms = jnp.concatenate([norm[:, r * BLOCK : (r + 1) * BLOCK] for r in range(NQ)], axis=0)
    for d in range(NQ):
        out[d, pl.ds(0, NQ), :] = norms
        out[d, pl.ds(NQ, NQ), :] = jnp.broadcast_to(pick[:, d * BLOCK : (d + 1) * BLOCK], (NQ, BLOCK))


def item_kernel(
    place, own, one, two, three, queries, stats,
    number_out, loss_out, item_out, gone_out, rows_all, live, shifts, gone, sems
):
    pieces = (own, one, two, three)
    number = list_live(place, pieces, rows_all, live, shifts)
    number_out[0] = number
    item_out[...] = jnp.zeros(item_out.shape, bf16)
    for k in range(NX):
        x = (place[2] - k) & (NX - 1)
        meta = pieces[k][pl.ds(SLOTS_DEV * BLOCK, META), :]
        for y in range(NY):
            item_out[y * NX + x, pl.ds(SLOTS_DEV * PART, META), :] = meta
    top = stats[0, pl.ds(0, NQ), :]
    pick = stats[0, pl.ds(NQ, NQ), :]
    for r in range(1, NQ):
        top = jnp.maximum(top, stats[r, pl.ds(0, NQ), :])
        pick = pick + stats[r, pl.ds(NQ, NQ), :]
    total = jnp.zeros_like(top)
    for r in range(NQ):
        total = total + jnp.exp(stats[r, pl.ds(0, NQ), :] - top)
    norms = top + jnp.log(total)
    mine = lax.broadcasted_iota(i32, norms.shape, 0) == place[1]
    loss_out[...] = jnp.sum(jnp.where(mine, norms - pick, 0.0), axis=0, keepdims=True)
    item_index = lax.broadcasted_iota(i32, (BLOCK, CHUNK), 0)

    def one_slot(i, carry):
        shift = shifts[i]
        rows = rows_all[i]
        slot = live[i]
        part = jnp.zeros((BLOCK, D), f32)
        for b in range(CHUNKS):
            target_slot, target_item = target_chunk(queries, b)
            wanted = jnp.where(target_slot == slot, target_item, -1)
            norm = jnp.concatenate([norms[2 * b : 2 * b + 1], norms[2 * b + 1 : 2 * b + 2]], axis=1)
            query_rows = query_chunk(queries, b)
            probs = jnp.exp(products(rows, query_rows) - (norm + shift))
            dlogit = jnp.where(item_index == wanted, probs - 1.0, probs).astype(bf16)
            gone[i, :, pl.ds(b * CHUNK, CHUNK)] = dlogit
            part = part + jnp.dot(dlogit, query_rows, preferred_element_type=f32)
        part = (logit_scale * part).astype(bf16)
        x = slot // (NQ * SLOTS_DEV)
        j = slot % SLOTS_DEV
        for y in range(NY):
            item_out[y * NX + x, pl.ds(pl.multiple_of(j * PART, PART), PART), :] = part[y * PART : (y + 1) * PART]
        pltpu.make_async_copy(gone.at[i], gone_out.at[i], sems.at[i]).start()
        return carry

    lax.fori_loop(0, number, one_slot, 0)

    def pad(i, carry):
        rows_all[i] = jnp.zeros((BLOCK, D), bf16)
        gone[i] = jnp.zeros((BLOCK, NQ * BLOCK), bf16)
        pltpu.make_async_copy(gone.at[i], gone_out.at[i], sems.at[i]).start()
        return carry

    padded = (number + TOGETHER - 1) // TOGETHER * TOGETHER
    lax.fori_loop(number, padded, pad, 0)

    def finish(i, carry):
        pltpu.make_async_copy(gone.at[i], gone_out.at[i], sems.at[i]).wait()
        return carry

    lax.fori_loop(0, padded, finish, 0)


def query_kernel(number, rows_all, gone_in, out, total, gone, sems):
    groups = (number[0] + TOGETHER - 1) // TOGETHER

    def fetch(g):
        some = pl.ds(g * TOGETHER, TOGETHER)
        return pltpu.make_async_copy(gone_in.at[some], gone.at[some], sems.at[g])

    def begin(g, carry):
        fetch(g).start()
        return carry

    lax.fori_loop(0, groups, begin, 0)
    total[...] = jnp.zeros(total.shape, f32)

    def one_group(g, carry):
        fetch(g).wait()
        some = pl.ds(g * TOGETHER, TOGETHER)
        rows = rows_all[some].reshape(TOGETHER * BLOCK, D).T
        for b in range(CHUNKS):
            cols = pl.ds(b * CHUNK, CHUNK)
            dlogit = gone[some, :, cols].reshape(TOGETHER * BLOCK, CHUNK)
            total[:, cols] = total[:, cols] + jnp.dot(rows, dlogit, preferred_element_type=f32)
        return carry

    lax.fori_loop(0, groups, one_group, 0)
    for r in range(NQ):
        out[r] = total[:, pl.ds(r * BLOCK, BLOCK)].astype(bf16)


def gather_parts_kernel(parts, out, total):
    lane = lax.broadcasted_iota(i32, (1, D), 1)
    total[...] = jnp.zeros(total.shape, f32)
    for y in range(NY):
        meta = parts[y * NX, pl.ds(SLOTS_DEV * PART, META), :].astype(f32)
        for j in range(SLOTS_DEV):
            block = jnp.sum(jnp.where(lane == j, meta[3:4], 0.0)).astype(i32)
            piece = jnp.zeros((PART, D), f32)
            for x in range(NX):
                piece = piece + parts[y * NX + x, pl.ds(j * PART, PART), :].astype(f32)
            total[block] = total[block] + piece
    out[...] = total[...].astype(bf16)


def adam_kernel(place, own, one, two, three, table, first, second, *rest):
    outs, results, sems = rest[:3], rest[3:6], rest[6]
    copies = []
    for b in range(BLOCKS_DEV):
        for k, piece in enumerate((own, one, two, three)):
            y = (place[3] - k) & (NY - 1)
            rows = pl.ds(pl.multiple_of(b * BLOCK + y * PART, PART), PART)
            grad = piece[b]
            first_new = beta_first * first[rows, :] + (1.0 - beta_first) * grad
            second_new = beta_second * second[rows, :] + (1.0 - beta_second) * grad * grad
            results[1][rows, :] = first_new
            results[2][rows, :] = second_new
            results[0][rows, :] = table[rows, :] - learn_rate * (first_new / bias_first) / (
                jnp.sqrt(second_new / bias_second) + adam_eps
            )
        block = pl.ds(b * BLOCK, BLOCK)
        for n in range(3):
            copy = pltpu.make_async_copy(results[n].at[block, :], outs[n].at[block, :], sems.at[b, n])
            copy.start()
            copies.append(copy)
    for copy in copies:
        copy.wait()


def query_sum_kernel(parts, out):
    total = parts[0].astype(f32)
    for r in range(1, NQ):
        total = total + parts[r].astype(f32)
    out[0] = total.T


def step(queries, targets, samp_ids, counts, logq, table, first_moment, second_moment):
    place = lax.axis_index("zl") * NC + lax.axis_index("c")
    own = lax.axis_index("c") * NZ + lax.axis_index("zl")
    where = jnp.stack([place, own, lax.axis_index("x"), lax.axis_index("y")]).astype(i32)
    item_shape = jax.ShapeDtypeStruct((SLOTS_DEV * BLOCK + META, D), bf16)
    items, query_rows = pl.pallas_call(
        pack_kernel,
        out_shape=(item_shape, jax.ShapeDtypeStruct((NZ, BLOCK + META, D), bf16)),
        in_specs=[smem(), smem(), smem(), hbm(), vmem(), vmem()],
        out_specs=(vmem(), vmem()),
        scratch_shapes=[pltpu.VMEM((SLOTS_DEV, BLOCK, D), f32), pltpu.SemaphoreType.DMA((SLOTS_DEV,))],
        name="pack",
    )(samp_ids, counts, logq, table, queries, targets)

    every_query = lax.all_to_all(query_rows, "zl", 0, 0, tiled=True)
    pieces = [items]
    for k in range(1, NX):
        pieces.append(lax.ppermute(items, "x", [(i, (i + k) % NX) for i in range(NX)]))
    every_query = lax.all_gather(every_query, "c", axis=0, tiled=True)

    tables = [pltpu.SMEM((SLOTS + 1,), i32), pltpu.SMEM((SLOTS + 1,), f32)]
    rows_spec = pltpu.VMEM((SLOTS + 1, BLOCK, D), bf16)
    stats = pl.pallas_call(
        totals_kernel,
        out_shape=jax.ShapeDtypeStruct((NQ, 2 * NQ, BLOCK), f32),
        in_specs=[smem()] + [vmem()] * (NX + 1),
        out_specs=vmem(),
        scratch_shapes=[rows_spec] + tables + [pltpu.VMEM((1, NQ * BLOCK), f32)] + [pltpu.VMEM((8, NQ * BLOCK), f32)] * 3,
        compiler_params=limit(10),
        name="totals",
    )(where, *pieces, every_query)
    stats = lax.all_to_all(stats, QROWS, 0, 0, tiled=True)

    number, loss, item_parts, gone, rows_all = pl.pallas_call(
        item_kernel,
        out_shape=(
            jax.ShapeDtypeStruct((1,), i32),
            jax.ShapeDtypeStruct((1, BLOCK), f32),
            jax.ShapeDtypeStruct((NY * NX, SLOTS_DEV * PART + META, D), bf16),
            jax.ShapeDtypeStruct((SLOTS, BLOCK, NQ * BLOCK), bf16),
            jax.ShapeDtypeStruct((SLOTS + 1, BLOCK, D), bf16),
        ),
        in_specs=[smem()] + [vmem()] * (NX + 2),
        out_specs=(smem(), vmem(), vmem(), hbm(), vmem()),
        scratch_shapes=tables
        + [pltpu.VMEM((SLOTS, BLOCK, NQ * BLOCK), bf16), pltpu.SemaphoreType.DMA((SLOTS,))],
        compiler_params=limit(16),
        name="items",
    )(where, *pieces, every_query, stats)

    item_parts = lax.all_to_all(item_parts, ("y", "x"), 0, 0, tiled=True)
    query_parts = pl.pallas_call(
        query_kernel,
        out_shape=jax.ShapeDtypeStruct((NQ, D, BLOCK), bf16),
        in_specs=[smem(), vmem(), hbm()],
        out_specs=vmem(),
        scratch_shapes=[
            pltpu.VMEM((D, NQ * BLOCK), f32),
            pltpu.VMEM((SLOTS, BLOCK, NQ * BLOCK), bf16),
            pltpu.SemaphoreType.DMA((SLOTS // TOGETHER,)),
        ],
        compiler_params=limit(12),
        cost_estimate=pl.CostEstimate(flops=1 << 30, bytes_accessed=6 << 20, transcendentals=0),
        name="query_parts",
    )(number, rows_all, gone)
    part = pl.pallas_call(
        gather_parts_kernel,
        out_shape=jax.ShapeDtypeStruct((BLOCKS_DEV, PART, D), bf16),
        in_specs=[vmem()],
        out_specs=vmem(),
        scratch_shapes=[pltpu.VMEM((BLOCKS_DEV, PART, D), f32)],
        compiler_params=limit(4),
        name="gather_parts",
    )(item_parts)
    other = lax.ppermute(part, "zh", [(0, 1), (1, 0), (2, 3), (3, 2)])
    part = lax.optimization_barrier((part.astype(f32) + other.astype(f32)).astype(bf16))
    other = lax.ppermute(part, "zh", [(1, 2), (2, 1), (3, 0), (0, 3)])
    part = part.astype(f32) + other.astype(f32)
    query_parts = lax.all_to_all(query_parts, QROWS, 0, 0, tiled=True)
    query_grad = pl.pallas_call(
        query_sum_kernel,
        out_shape=jax.ShapeDtypeStruct((1, BLOCK, D), f32),
        in_specs=[vmem()],
        out_specs=vmem(),
        compiler_params=limit(4),
        name="query_sum",
    )(query_parts)
    grads = [part]
    for k in range(1, NY):
        grads.append(lax.ppermute(part, "y", [(i, (i + k) % NY) for i in range(NY)]))

    new_table, new_first, new_second = pl.pallas_call(
        adam_kernel,
        out_shape=(jax.ShapeDtypeStruct(table.shape, f32),) * 3,
        in_specs=[smem()] + [vmem()] * (NY + 3),
        out_specs=(hbm(),) * 3,
        scratch_shapes=[pltpu.VMEM(table.shape, f32)] * 3 + [pltpu.SemaphoreType.DMA((BLOCKS_DEV, 3))],
        compiler_params=limit(12),
        name="adam",
    )(where, *grads, table, first_moment, second_moment)
    return loss, query_grad, new_table, new_first, new_second


def solution(mesh):
    fine = Mesh(mesh.devices.reshape(4, NY, NX, NZ, NC), ("zh", "y", "x", "zl", "c"))
    rep = ("zh", "y")
    shard = ("x", "zl", "c")
    in_specs = (
        P(rep, shard, None),
        P(rep, shard),
        P(rep, shard),
        P(rep, shard),
        P(rep, shard),
        P(shard, None),
        P(shard, None),
        P(shard, None),
    )
    out_specs = (
        P(rep, shard),
        P(rep, shard, None),
        P(shard, None),
        P(shard, None),
        P(shard, None),
    )
    return jax.shard_map(step, mesh=fine, in_specs=in_specs, out_specs=out_specs, check_vma=False)
```

```python
import jax
import jax.numpy as jnp
from jax import lax
from jax.experimental import pallas as pl
from jax.experimental.pallas import tpu as pltpu
from jax.sharding import Mesh, PartitionSpec as P


BLOCK = 128
D = 256
SLOTS_DEV = 4
BLOCKS_DEV = 6
NX = 4
NY = 4
NZ = 4
NC = 2
NQ = NZ * NC
SLOTS = NX * SLOTS_DEV
PART = BLOCK // NY
META = 16
CHUNK = 256
CHUNKS = NQ * BLOCK // CHUNK
TOGETHER = 4
QROWS = ("c", "zl")

logit_scale = 2.0
beta_first = 0.9
beta_second = 0.99
learn_rate = 0.01
adam_eps = 1e-08
bias_first = 1.0 - 0.9**10
bias_second = 1.0 - 0.99**10
floor_value = -1e30

f32 = jnp.float32
bf16 = jnp.bfloat16
i32 = jnp.int32


def vmem():
    return pl.BlockSpec(memory_space=pltpu.VMEM)


def hbm():
    return pl.BlockSpec(memory_space=pltpu.HBM)


def smem():
    return pl.BlockSpec(memory_space=pltpu.SMEM)


def limit(mib):
    return pltpu.CompilerParams(vmem_limit_bytes=mib << 20)


def pack_kernel(ids, count, logq, table, queries, targets, item_out, query_out):
    slot = (targets[...] >> 7).astype(f32)
    item = (targets[...] & (BLOCK - 1)).astype(f32)
    both = jnp.broadcast_to(jnp.concatenate([slot, item], axis=1), (META, D)).astype(bf16)
    for z in range(NZ):
        query_out[z, pl.ds(0, BLOCK), :] = queries[0]
        query_out[z, pl.ds(BLOCK, META), :] = both
    row = lax.broadcasted_iota(i32, (META, D), 0)
    lane = lax.broadcasted_iota(i32, (META, D), 1)
    meta = jnp.where(row == 4, count[0, 0].astype(f32), 0.0)
    for j in range(SLOTS_DEV):
        whole = jnp.full((META, D), logq[0, j], f32)
        high = whole.astype(bf16).astype(f32)
        mid = (whole - high).astype(bf16).astype(f32)
        low = whole - high - mid
        ident = jnp.full((META, D), ids[0, j].astype(f32), f32)
        value = jnp.where(row == 0, high, jnp.where(row == 1, mid, jnp.where(row == 2, low, ident)))
        meta = jnp.where((lane == j) & (row < 4), value, meta)
    item_out[pl.ds(SLOTS_DEV * BLOCK, META), :] = meta.astype(bf16)
    for j in range(SLOTS_DEV):
        rows = table[pl.ds(pl.multiple_of(ids[0, j] * BLOCK, BLOCK), BLOCK), :]
        item_out[pl.ds(j * BLOCK, BLOCK), :] = (logit_scale * rows.astype(bf16).astype(f32)).astype(bf16)


def query_chunk(queries, b):
    return jnp.concatenate([queries[2 * b, pl.ds(0, BLOCK), :], queries[2 * b + 1, pl.ds(0, BLOCK), :]], axis=0)


def target_codes(queries):
    parts = []
    for r in range(NQ):
        row = queries[r, pl.ds(BLOCK, META), :].astype(f32)[0:1]
        parts.append((row[:, :BLOCK] * BLOCK + row[:, BLOCK:]).astype(i32))
    return jnp.concatenate(parts, axis=1)


def totals_kernel(
    place, own, one, two, three, queries,
    out, rows_all, metas, live, shifts, scores, tops, sums,
):
    lane = lax.broadcasted_iota(i32, (1, D), 1)
    number = jnp.int32(0)
    for k, piece in enumerate((own, one, two, three)):
        x = (place[2] - k) & (NX - 1)
        raw = piece[pl.ds(SLOTS_DEV * BLOCK, META), :]
        metas[x] = raw
        meta = raw.astype(f32)
        row = meta[0:1] + meta[1:2] + meta[2:3]
        count = jnp.max(meta[4:5]).astype(i32)
        for j in range(SLOTS_DEV):
            shifts[number] = jnp.sum(jnp.where(lane == j, row, 0.0))
            live[number] = x * (NQ * SLOTS_DEV) + place[0] * SLOTS_DEV + j
            rows_all[number] = piece[pl.ds(j * BLOCK, BLOCK), :]
            number = number + (j < count).astype(i32)
    live[SLOTS + 1] = number

    def pad(i, carry):
        rows_all[i] = jnp.zeros((BLOCK, D), bf16)
        shifts[i] = -floor_value
        live[i] = -1
        return carry

    lax.fori_loop(number, (number + TOGETHER - 1) // TOGETHER * TOGETHER, pad, 0)
    pairs = (number + 1) // 2
    tops[...] = jnp.full(tops.shape, floor_value, f32)
    sums[...] = jnp.zeros(sums.shape, f32)

    def score(p, carry):
        rows = rows_all[pl.ds(2 * p, 2)].reshape(2 * BLOCK, D)
        for b in range(CHUNKS):
            cols = pl.ds(b * CHUNK, CHUNK)
            doubled = pair_products(rows, queries, b)
            top = tops[:, cols]
            for h in range(2):
                half = doubled[h * BLOCK : (h + 1) * BLOCK]
                scores[2 * p + h, :, cols] = half
                top = jnp.maximum(top, jnp.max(half.reshape(BLOCK // 8, 8, CHUNK), axis=0) - shifts[2 * p + h])
            tops[:, cols] = top
        return carry

    lax.fori_loop(0, pairs, score, 0)
    top_row = jnp.max(tops[...], axis=0, keepdims=True)

    def weigh(p, carry):
        for h in range(2):
            i = 2 * p + h
            for b in range(CHUNKS):
                cols = pl.ds(b * CHUNK, CHUNK)
                base = top_row[:, b * CHUNK : (b + 1) * CHUNK] + shifts[i]
                weight = jnp.exp(scores[i, :, cols] - base)
                sums[:, cols] = sums[:, cols] + jnp.sum(weight.reshape(BLOCK // 8, 8, CHUNK), axis=0)
        return carry

    lax.fori_loop(0, pairs, weigh, 0)
    norm = top_row + jnp.log(jnp.sum(sums[...], axis=0, keepdims=True))
    norms = jnp.concatenate([norm[:, r * BLOCK : (r + 1) * BLOCK] for r in range(NQ)], axis=0)
    for d in range(NQ):
        out[d] = norms


def pair_products(rows, queries, b):
    return lax.dot_general(rows, query_chunk(queries, b), (((1,), (1,)), ((), ())), preferred_element_type=f32)


def dlogits(doubled, norm, codes, live, shifts, i):
    probs = jnp.exp(doubled - (norm + shifts[i]))
    item_index = lax.broadcasted_iota(i32, (BLOCK, CHUNK), 0)
    return jnp.where(item_index == codes - live[i] * BLOCK, probs - 1.0, probs).astype(bf16)


def item_kernel(place, live, shifts, rows_all, metas, queries, stats, item_out, norm_out, held):
    top = stats[0]
    for r in range(1, NQ):
        top = jnp.maximum(top, stats[r])
    total = jnp.zeros_like(top)
    for r in range(NQ):
        total = total + jnp.exp(stats[r] - top)
    norms = top + jnp.log(total)
    norm_row = jnp.concatenate([norms[r : r + 1] for r in range(NQ)], axis=1)
    norm_out[...] = norm_row
    codes = target_codes(queries)
    item_out[...] = jnp.zeros(item_out.shape, bf16)
    for x in range(NX):
        for y in range(NY):
            item_out[y * NX + x, pl.ds(SLOTS_DEV * PART, META), :] = metas[x]
    number = live[SLOTS + 1]

    def one_pair(p, carry):
        rows = rows_all[pl.ds(2 * p, 2)].reshape(2 * BLOCK, D)
        for b in range(CHUNKS):
            doubled = pair_products(rows, queries, b)
            norm = norm_row[:, b * CHUNK : (b + 1) * CHUNK]
            code = codes[:, b * CHUNK : (b + 1) * CHUNK]
            for h in range(2):
                half = pl.ds(h * BLOCK, BLOCK)
                held[half, pl.ds(b * CHUNK, CHUNK)] = dlogits(
                    doubled[h * BLOCK : (h + 1) * BLOCK], norm, code, live, shifts, 2 * p + h
                )
        every = jnp.concatenate([query_chunk(queries, b) for b in range(CHUNKS)], axis=0)
        total = jnp.dot(held[...], every, preferred_element_type=f32)
        for h in range(2):
            i = 2 * p + h
            part = (logit_scale * total[h * BLOCK : (h + 1) * BLOCK]).astype(bf16)

            @pl.when(i < number)
            def _():
                x = live[i] // (NQ * SLOTS_DEV)
                rows = pl.ds(pl.multiple_of(live[i] % SLOTS_DEV * PART, PART), PART)
                for y in range(NY):
                    item_out[y * NX + x, rows, :] = part[y * PART : (y + 1) * PART]

        return carry

    lax.fori_loop(0, (number + 1) // 2, one_pair, 0)


def query_kernel(live, shifts, rows_all, queries, norms, out, total, picks, taken):
    codes = target_codes(queries)
    norm_row = norms[...]
    total[...] = jnp.zeros(total.shape, f32)
    picks[...] = jnp.zeros(picks.shape, f32)
    taken[...] = jnp.zeros(taken.shape, f32)
    item_index = lax.broadcasted_iota(i32, (BLOCK, CHUNK), 0)

    def one_group(g, carry):
        rows = rows_all[pl.ds(g * TOGETHER, TOGETHER)].reshape(TOGETHER * BLOCK, D)
        turned = rows.T
        for b in range(CHUNKS):
            cols = pl.ds(b * CHUNK, CHUNK)
            doubled = pair_products(rows, queries, b)
            norm = norm_row[:, b * CHUNK : (b + 1) * CHUNK]
            code = codes[:, b * CHUNK : (b + 1) * CHUNK]
            parts = []
            for h in range(TOGETHER):
                i = g * TOGETHER + h
                block = doubled[h * BLOCK : (h + 1) * BLOCK]
                wanted = code - live[i] * BLOCK
                match = item_index == wanted
                marked = jnp.where(match, block, 0.0)
                picks[:, cols] = picks[:, cols] + jnp.sum(marked.reshape(BLOCK // 8, 8, CHUNK), axis=0)
                here = (wanted >= 0) & (wanted < BLOCK)
                taken[:, cols] = taken[:, cols] + jnp.where(here, shifts[i], 0.0)
                probs = jnp.exp(block - (norm + shifts[i]))
                parts.append(jnp.where(match, probs - 1.0, probs).astype(bf16))
            total[:, cols] = total[:, cols] + jnp.dot(
                turned, jnp.concatenate(parts, axis=0), preferred_element_type=f32
            )
        return carry

    lax.fori_loop(0, (live[SLOTS + 1] + TOGETHER - 1) // TOGETHER, one_group, 0)
    row = lax.broadcasted_iota(i32, (META, BLOCK), 0)
    for r in range(NQ):
        cols = pl.ds(r * BLOCK, BLOCK)
        out[r, pl.ds(0, D), :] = total[:, cols].astype(bf16)
        pick = jnp.sum(picks[:, cols], axis=0, keepdims=True) - taken[:, cols]
        pick = jnp.broadcast_to(pick, (META, BLOCK))
        high = pick.astype(bf16).astype(f32)
        mid = (pick - high).astype(bf16).astype(f32)
        low = pick - high - mid
        three = jnp.where(row == 0, high, jnp.where(row == 1, mid, jnp.where(row == 2, low, 0.0)))
        out[r, pl.ds(D, META), :] = three.astype(bf16)


def gather_parts_kernel(parts, out, total):
    lane = lax.broadcasted_iota(i32, (1, D), 1)
    total[...] = jnp.zeros(total.shape, f32)
    for y in range(NY):
        meta = parts[y * NX, pl.ds(SLOTS_DEV * PART, META), :].astype(f32)
        for j in range(SLOTS_DEV):
            block = jnp.sum(jnp.where(lane == j, meta[3:4], 0.0)).astype(i32)
            piece = jnp.zeros((PART, D), f32)
            for x in range(NX):
                piece = piece + parts[y * NX + x, pl.ds(j * PART, PART), :].astype(f32)
            total[block] = total[block] + piece
    out[...] = total[...].astype(bf16)


def adam_kernel(place, own, one, two, three, table, first, second, *rest):
    outs, results, sems = rest[:3], rest[3:6], rest[6]
    copies = []
    for b in range(BLOCKS_DEV):
        for k, piece in enumerate((own, one, two, three)):
            y = (place[3] - k) & (NY - 1)
            rows = pl.ds(pl.multiple_of(b * BLOCK + y * PART, PART), PART)
            grad = piece[b]
            first_new = beta_first * first[rows, :] + (1.0 - beta_first) * grad
            second_new = beta_second * second[rows, :] + (1.0 - beta_second) * grad * grad
            results[1][rows, :] = first_new
            results[2][rows, :] = second_new
            results[0][rows, :] = table[rows, :] - learn_rate * (first_new / bias_first) / (
                jnp.sqrt(second_new / bias_second) + adam_eps
            )
        block = pl.ds(b * BLOCK, BLOCK)
        for n in range(3):
            copy = pltpu.make_async_copy(results[n].at[block, :], outs[n].at[block, :], sems.at[b, n])
            copy.start()
            copies.append(copy)
    for copy in copies:
        copy.wait()


def query_sum_kernel(place, norms, parts, loss_out, out):
    total = parts[0].astype(f32)
    for r in range(1, NQ):
        total = total + parts[r].astype(f32)
    out[0] = total[:D].T
    pick = jnp.sum(total[D : D + META], axis=0, keepdims=True)
    loss_out[...] = norms[:, pl.ds(pl.multiple_of(place[1] * BLOCK, BLOCK), BLOCK)] - pick


def step(queries, targets, samp_ids, counts, logq, table, first_moment, second_moment):
    place = lax.axis_index("zl") * NC + lax.axis_index("c")
    own = lax.axis_index("c") * NZ + lax.axis_index("zl")
    where = jnp.stack([place, own, lax.axis_index("x"), lax.axis_index("y")]).astype(i32)
    item_shape = jax.ShapeDtypeStruct((SLOTS_DEV * BLOCK + META, D), bf16)
    items, query_rows = pl.pallas_call(
        pack_kernel,
        out_shape=(item_shape, jax.ShapeDtypeStruct((NZ, BLOCK + META, D), bf16)),
        in_specs=[smem(), smem(), smem(), vmem(), vmem(), vmem()],
        out_specs=(vmem(), vmem()),
        name="pack",
    )(samp_ids, counts, logq, table, queries, targets)

    every_query = lax.all_to_all(query_rows, "zl", 0, 0, tiled=True)
    pieces = [items]
    for k in range(1, NX):
        pieces.append(lax.ppermute(items, "x", [(i, (i + k) % NX) for i in range(NX)]))
    every_query = lax.all_gather(every_query, "c", axis=0, tiled=True)

    wide = NQ * BLOCK
    stats, rows_all, metas, live, shifts = pl.pallas_call(
        totals_kernel,
        out_shape=(
            jax.ShapeDtypeStruct((NQ, NQ, BLOCK), f32),
            jax.ShapeDtypeStruct((SLOTS + 1, BLOCK, D), bf16),
            jax.ShapeDtypeStruct((NX, META, D), bf16),
            jax.ShapeDtypeStruct((SLOTS + 2,), i32),
            jax.ShapeDtypeStruct((SLOTS + 1,), f32),
        ),
        in_specs=[smem()] + [vmem()] * (NX + 1),
        out_specs=(vmem(),) * 3 + (smem(), smem()),
        scratch_shapes=[pltpu.VMEM((SLOTS, BLOCK, wide), f32)]
        + [pltpu.VMEM((8, wide), f32)] * 2,
        compiler_params=limit(16),
        name="totals",
    )(where, *pieces, every_query)
    stats = lax.all_to_all(stats, QROWS, 0, 0, tiled=True)
    item_parts, norms = pl.pallas_call(
        item_kernel,
        out_shape=(
            jax.ShapeDtypeStruct((NY * NX, SLOTS_DEV * PART + META, D), bf16),
            jax.ShapeDtypeStruct((1, wide), f32),
        ),
        in_specs=[smem()] * 3 + [vmem()] * 4,
        out_specs=(vmem(),) * 2,
        scratch_shapes=[pltpu.VMEM((2 * BLOCK, wide), bf16)],
        compiler_params=limit(12),
        name="items",
    )(where, live, shifts, rows_all, metas, every_query, stats)

    item_parts = lax.all_to_all(item_parts, ("y", "x"), 0, 0, tiled=True)
    query_parts = pl.pallas_call(
        query_kernel,
        out_shape=jax.ShapeDtypeStruct((NQ, D + META, BLOCK), bf16),
        in_specs=[smem(), smem()] + [vmem()] * 3,
        out_specs=vmem(),
        scratch_shapes=[pltpu.VMEM((D, wide), f32), pltpu.VMEM((8, wide), f32), pltpu.VMEM((1, wide), f32)],
        compiler_params=limit(8),
        cost_estimate=pl.CostEstimate(flops=1 << 31, bytes_accessed=6 << 20, transcendentals=0),
        name="query_parts",
    )(live, shifts, rows_all, every_query, norms)
    part = pl.pallas_call(
        gather_parts_kernel,
        out_shape=jax.ShapeDtypeStruct((BLOCKS_DEV, PART, D), bf16),
        in_specs=[vmem()],
        out_specs=vmem(),
        scratch_shapes=[pltpu.VMEM((BLOCKS_DEV, PART, D), f32)],
        compiler_params=limit(4),
        name="gather_parts",
    )(item_parts)
    other = lax.ppermute(part, "zh", [(0, 1), (1, 0), (2, 3), (3, 2)])
    part = lax.optimization_barrier((part.astype(f32) + other.astype(f32)).astype(bf16))
    other = lax.ppermute(part, "zh", [(1, 2), (2, 1), (3, 0), (0, 3)])
    part = part.astype(f32) + other.astype(f32)
    query_parts = lax.all_to_all(query_parts, QROWS, 0, 0, tiled=True)
    loss, query_grad = pl.pallas_call(
        query_sum_kernel,
        out_shape=(jax.ShapeDtypeStruct((1, BLOCK), f32), jax.ShapeDtypeStruct((1, BLOCK, D), f32)),
        in_specs=[smem(), vmem(), vmem()],
        out_specs=(vmem(), vmem()),
        compiler_params=limit(4),
        name="query_sum",
    )(where, norms, query_parts)
    grads = [part]
    for k in range(1, NY):
        grads.append(lax.ppermute(part, "y", [(i, (i + k) % NY) for i in range(NY)]))

    new_table, new_first, new_second = pl.pallas_call(
        adam_kernel,
        out_shape=(jax.ShapeDtypeStruct(table.shape, f32),) * 3,
        in_specs=[smem()] + [vmem()] * (NY + 3),
        out_specs=(hbm(),) * 3,
        scratch_shapes=[pltpu.VMEM(table.shape, f32)] * 3 + [pltpu.SemaphoreType.DMA((BLOCKS_DEV, 3))],
        compiler_params=limit(12),
        name="adam",
    )(where, *grads, table, first_moment, second_moment)
    return loss, query_grad, new_table, new_first, new_second


def solution(mesh):
    fine = Mesh(mesh.devices.reshape(4, NY, NX, NZ, NC), ("zh", "y", "x", "zl", "c"))
    rep = ("zh", "y")
    shard = ("x", "zl", "c")
    in_specs = (
        P(rep, shard, None),
        P(rep, shard),
        P(rep, shard),
        P(rep, shard),
        P(rep, shard),
        P(shard, None),
        P(shard, None),
        P(shard, None),
    )
    out_specs = (
        P(rep, shard),
        P(rep, shard, None),
        P(shard, None),
        P(shard, None),
        P(shard, None),
    )
    return jax.shard_map(step, mesh=fine, in_specs=in_specs, out_specs=out_specs, check_vma=False)
```

```python
import jax
import jax.numpy as jnp
from jax import lax
from jax.experimental import pallas as pl
from jax.experimental.pallas import tpu as pltpu
from jax.sharding import Mesh, PartitionSpec as P


BLOCK = 128
D = 256
SLOTS_DEV = 4
BLOCKS_DEV = 6
NX = 4
NY = 4
NZ = 4
NC = 2
NQ = NZ * NC
SLOTS = NX * SLOTS_DEV
PART = BLOCK // NY
META = 16
CHUNK = 256
CHUNKS = NQ * BLOCK // CHUNK
TOGETHER = 4
QROWS = ("c", "zl")

logit_scale = 2.0
beta_first = 0.9
beta_second = 0.99
learn_rate = 0.01
adam_eps = 1e-08
bias_first = 1.0 - 0.9**10
bias_second = 1.0 - 0.99**10
floor_value = -1e30

f32 = jnp.float32
bf16 = jnp.bfloat16
i32 = jnp.int32


def vmem():
    return pl.BlockSpec(memory_space=pltpu.VMEM)


def hbm():
    return pl.BlockSpec(memory_space=pltpu.HBM)


def smem():
    return pl.BlockSpec(memory_space=pltpu.SMEM)


def limit(mib):
    return pltpu.CompilerParams(vmem_limit_bytes=mib << 20)


def pack_kernel(ids, count, logq, table, queries, targets, item_out, query_out):
    slot = (targets[...] >> 7).astype(f32)
    item = (targets[...] & (BLOCK - 1)).astype(f32)
    both = jnp.broadcast_to(jnp.concatenate([slot, item], axis=1), (META, D)).astype(bf16)
    for z in range(NZ):
        query_out[z, pl.ds(0, BLOCK), :] = queries[0]
        query_out[z, pl.ds(BLOCK, META), :] = both
    row = lax.broadcasted_iota(i32, (META, D), 0)
    lane = lax.broadcasted_iota(i32, (META, D), 1)
    meta = jnp.where(row == 4, count[0, 0].astype(f32), 0.0)
    for j in range(SLOTS_DEV):
        whole = jnp.full((META, D), logq[0, j], f32)
        high = whole.astype(bf16).astype(f32)
        mid = (whole - high).astype(bf16).astype(f32)
        low = whole - high - mid
        ident = jnp.full((META, D), ids[0, j].astype(f32), f32)
        value = jnp.where(row == 0, high, jnp.where(row == 1, mid, jnp.where(row == 2, low, ident)))
        meta = jnp.where((lane == j) & (row < 4), value, meta)
    item_out[pl.ds(SLOTS_DEV * BLOCK, META), :] = meta.astype(bf16)
    for j in range(SLOTS_DEV):
        rows = table[pl.ds(pl.multiple_of(ids[0, j] * BLOCK, BLOCK), BLOCK), :]
        item_out[pl.ds(j * BLOCK, BLOCK), :] = (logit_scale * rows.astype(bf16).astype(f32)).astype(bf16)


def query_chunk(queries, b):
    return jnp.concatenate([queries[2 * b, pl.ds(0, BLOCK), :], queries[2 * b + 1, pl.ds(0, BLOCK), :]], axis=0)


def target_codes(queries):
    parts = []
    for r in range(NQ):
        row = queries[r, pl.ds(BLOCK, META), :].astype(f32)[0:1]
        parts.append((row[:, :BLOCK] * BLOCK + row[:, BLOCK:]).astype(i32))
    return jnp.concatenate(parts, axis=1)


def totals_kernel(
    place, own, one, two, three, queries,
    out, rows_all, metas, live, shifts, scores, tops, sums,
):
    lane = lax.broadcasted_iota(i32, (1, D), 1)
    number = jnp.int32(0)
    for k, piece in enumerate((own, one, two, three)):
        x = (place[2] - k) & (NX - 1)
        raw = piece[pl.ds(SLOTS_DEV * BLOCK, META), :]
        metas[x] = raw
        meta = raw.astype(f32)
        row = meta[0:1] + meta[1:2] + meta[2:3]
        count = jnp.max(meta[4:5]).astype(i32)
        for j in range(SLOTS_DEV):
            shifts[number] = jnp.sum(jnp.where(lane == j, row, 0.0))
            live[number] = x * (NQ * SLOTS_DEV) + place[0] * SLOTS_DEV + j
            rows_all[number] = piece[pl.ds(j * BLOCK, BLOCK), :]
            number = number + (j < count).astype(i32)
    live[SLOTS + 1] = number

    def pad(i, carry):
        rows_all[i] = jnp.zeros((BLOCK, D), bf16)
        shifts[i] = -floor_value
        live[i] = -1
        return carry

    lax.fori_loop(number, (number + TOGETHER - 1) // TOGETHER * TOGETHER, pad, 0)
    pairs = (number + 1) // 2
    tops[...] = jnp.full(tops.shape, floor_value, f32)
    sums[...] = jnp.zeros(sums.shape, f32)

    def score(p, carry):
        rows = rows_all[pl.ds(2 * p, 2)].reshape(2 * BLOCK, D)
        for b in range(CHUNKS):
            cols = pl.ds(b * CHUNK, CHUNK)
            doubled = pair_products(rows, queries, b)
            top = tops[:, cols]
            for h in range(2):
                half = doubled[h * BLOCK : (h + 1) * BLOCK]
                scores[2 * p + h, :, cols] = half
                top = jnp.maximum(top, jnp.max(half.reshape(BLOCK // 8, 8, CHUNK), axis=0) - shifts[2 * p + h])
            tops[:, cols] = top
        return carry

    lax.fori_loop(0, pairs, score, 0)
    top_row = jnp.max(tops[...], axis=0, keepdims=True)

    def weigh(p, carry):
        for h in range(2):
            i = 2 * p + h
            for b in range(CHUNKS):
                cols = pl.ds(b * CHUNK, CHUNK)
                base = top_row[:, b * CHUNK : (b + 1) * CHUNK] + shifts[i]
                weight = jnp.exp(scores[i, :, cols] - base)
                sums[:, cols] = sums[:, cols] + jnp.sum(weight.reshape(BLOCK // 8, 8, CHUNK), axis=0)
        return carry

    lax.fori_loop(0, pairs, weigh, 0)
    norm = top_row + jnp.log(jnp.sum(sums[...], axis=0, keepdims=True))
    norms = jnp.concatenate([norm[:, r * BLOCK : (r + 1) * BLOCK] for r in range(NQ)], axis=0)
    for d in range(NQ):
        out[d] = norms


def pair_products(rows, queries, b):
    return lax.dot_general(rows, query_chunk(queries, b), (((1,), (1,)), ((), ())), preferred_element_type=f32)


def dlogits(doubled, norm, codes, live, shifts, i):
    probs = jnp.exp(doubled - (norm + shifts[i]))
    item_index = lax.broadcasted_iota(i32, (BLOCK, CHUNK), 0)
    return jnp.where(item_index == codes - live[i] * BLOCK, probs - 1.0, probs).astype(bf16)


def item_kernel(place, live, shifts, rows_all, metas, queries, stats, item_out, norm_out, held):
    top = stats[0]
    for r in range(1, NQ):
        top = jnp.maximum(top, stats[r])
    total = jnp.zeros_like(top)
    for r in range(NQ):
        total = total + jnp.exp(stats[r] - top)
    norms = top + jnp.log(total)
    norm_row = jnp.concatenate([norms[r : r + 1] for r in range(NQ)], axis=1)
    norm_out[...] = norm_row
    codes = target_codes(queries)
    item_out[...] = jnp.zeros(item_out.shape, bf16)
    for x in range(NX):
        for y in range(NY):
            item_out[y * NX + x, pl.ds(SLOTS_DEV * PART, META), :] = metas[x]
    number = live[SLOTS + 1]

    def one_pair(p, carry):
        rows = rows_all[pl.ds(2 * p, 2)].reshape(2 * BLOCK, D)
        for b in range(CHUNKS):
            doubled = pair_products(rows, queries, b)
            norm = norm_row[:, b * CHUNK : (b + 1) * CHUNK]
            code = codes[:, b * CHUNK : (b + 1) * CHUNK]
            for h in range(2):
                half = pl.ds(h * BLOCK, BLOCK)
                held[half, pl.ds(b * CHUNK, CHUNK)] = dlogits(
                    doubled[h * BLOCK : (h + 1) * BLOCK], norm, code, live, shifts, 2 * p + h
                )
        every = jnp.concatenate([query_chunk(queries, b) for b in range(CHUNKS)], axis=0)
        total = jnp.dot(held[...], every, preferred_element_type=f32)
        for h in range(2):
            i = 2 * p + h
            part = (logit_scale * total[h * BLOCK : (h + 1) * BLOCK]).astype(bf16)

            @pl.when(i < number)
            def _():
                x = live[i] // (NQ * SLOTS_DEV)
                rows = pl.ds(pl.multiple_of(live[i] % SLOTS_DEV * PART, PART), PART)
                for y in range(NY):
                    item_out[y * NX + x, rows, :] = part[y * PART : (y + 1) * PART]

        return carry

    lax.fori_loop(0, (number + 1) // 2, one_pair, 0)


def query_kernel(live, shifts, rows_all, queries, norms, out, total, picks, taken):
    codes = target_codes(queries)
    norm_row = norms[...]
    total[...] = jnp.zeros(total.shape, f32)
    picks[...] = jnp.zeros(picks.shape, f32)
    taken[...] = jnp.zeros(taken.shape, f32)
    item_index = lax.broadcasted_iota(i32, (BLOCK, CHUNK), 0)

    def one_group(g, carry):
        rows = rows_all[pl.ds(g * TOGETHER, TOGETHER)].reshape(TOGETHER * BLOCK, D)
        turned = rows.T
        for b in range(CHUNKS):
            cols = pl.ds(b * CHUNK, CHUNK)
            doubled = pair_products(rows, queries, b)
            norm = norm_row[:, b * CHUNK : (b + 1) * CHUNK]
            code = codes[:, b * CHUNK : (b + 1) * CHUNK]
            parts = []
            for h in range(TOGETHER):
                i = g * TOGETHER + h
                block = doubled[h * BLOCK : (h + 1) * BLOCK]
                wanted = code - live[i] * BLOCK
                match = item_index == wanted
                marked = jnp.where(match, block, 0.0)
                picks[:, cols] = picks[:, cols] + jnp.sum(marked.reshape(BLOCK // 8, 8, CHUNK), axis=0)
                here = (wanted >= 0) & (wanted < BLOCK)
                taken[:, cols] = taken[:, cols] + jnp.where(here, shifts[i], 0.0)
                probs = jnp.exp(block - (norm + shifts[i]))
                parts.append(jnp.where(match, probs - 1.0, probs).astype(bf16))
            total[:, cols] = total[:, cols] + jnp.dot(
                turned, jnp.concatenate(parts, axis=0), preferred_element_type=f32
            )
        return carry

    lax.fori_loop(0, (live[SLOTS + 1] + TOGETHER - 1) // TOGETHER, one_group, 0)
    row = lax.broadcasted_iota(i32, (META, BLOCK), 0)
    for r in range(NQ):
        cols = pl.ds(r * BLOCK, BLOCK)
        out[r, pl.ds(0, D), :] = total[:, cols].astype(bf16)
        pick = jnp.sum(picks[:, cols], axis=0, keepdims=True) - taken[:, cols]
        pick = jnp.broadcast_to(pick, (META, BLOCK))
        high = pick.astype(bf16).astype(f32)
        mid = (pick - high).astype(bf16).astype(f32)
        low = pick - high - mid
        three = jnp.where(row == 0, high, jnp.where(row == 1, mid, jnp.where(row == 2, low, 0.0)))
        out[r, pl.ds(D, META), :] = three.astype(bf16)


def gather_parts_kernel(parts, out, total):
    lane = lax.broadcasted_iota(i32, (1, D), 1)
    total[...] = jnp.zeros(total.shape, f32)
    for y in range(NY):
        meta = parts[y * NX, pl.ds(SLOTS_DEV * PART, META), :].astype(f32)
        for j in range(SLOTS_DEV):
            block = jnp.sum(jnp.where(lane == j, meta[3:4], 0.0)).astype(i32)
            piece = jnp.zeros((PART, D), f32)
            for x in range(NX):
                piece = piece + parts[y * NX + x, pl.ds(j * PART, PART), :].astype(f32)
            total[block] = total[block] + piece
    out[...] = total[...].astype(bf16)


def adam_kernel(place, own, one, two, three, table, first, second, *rest):
    outs, results, sems = rest[:3], rest[3:6], rest[6]
    copies = []
    for b in range(BLOCKS_DEV):
        for k, piece in enumerate((own, one, two, three)):
            y = (place[3] - k) & (NY - 1)
            rows = pl.ds(pl.multiple_of(b * BLOCK + y * PART, PART), PART)
            grad = piece[b]
            first_new = beta_first * first[rows, :] + (1.0 - beta_first) * grad
            second_new = beta_second * second[rows, :] + (1.0 - beta_second) * grad * grad
            results[1][rows, :] = first_new
            results[2][rows, :] = second_new
            results[0][rows, :] = table[rows, :] - learn_rate * (first_new / bias_first) / (
                jnp.sqrt(second_new / bias_second) + adam_eps
            )
        block = pl.ds(b * BLOCK, BLOCK)
        for n in range(3):
            copy = pltpu.make_async_copy(results[n].at[block, :], outs[n].at[block, :], sems.at[b, n])
            copy.start()
            copies.append(copy)
    for copy in copies:
        copy.wait()


def query_sum_kernel(place, norms, parts, loss_out, out):
    total = parts[0].astype(f32)
    for r in range(1, NQ):
        total = total + parts[r].astype(f32)
    out[0] = total[:D].T
    pick = jnp.sum(total[D : D + META], axis=0, keepdims=True)
    loss_out[...] = norms[:, pl.ds(pl.multiple_of(place[1] * BLOCK, BLOCK), BLOCK)] - pick


def step(queries, targets, samp_ids, counts, logq, table, first_moment, second_moment):
    place = lax.axis_index("zl") * NC + lax.axis_index("c")
    own = lax.axis_index("c") * NZ + lax.axis_index("zl")
    where = jnp.stack([place, own, lax.axis_index("x"), lax.axis_index("y")]).astype(i32)
    item_shape = jax.ShapeDtypeStruct((SLOTS_DEV * BLOCK + META, D), bf16)
    items, query_rows = pl.pallas_call(
        pack_kernel,
        out_shape=(item_shape, jax.ShapeDtypeStruct((NZ, BLOCK + META, D), bf16)),
        in_specs=[smem(), smem(), smem(), vmem(), vmem(), vmem()],
        out_specs=(vmem(), vmem()),
        name="pack",
    )(samp_ids, counts, logq, table, queries, targets)

    every_query = lax.all_to_all(query_rows, "zl", 0, 0, tiled=True)
    pieces = [items]
    for k in range(1, NX):
        pieces.append(lax.ppermute(items, "x", [(i, (i + k) % NX) for i in range(NX)]))
    every_query = lax.all_gather(every_query, "c", axis=0, tiled=True)

    wide = NQ * BLOCK
    stats, rows_all, metas, live, shifts = pl.pallas_call(
        totals_kernel,
        out_shape=(
            jax.ShapeDtypeStruct((NQ, NQ, BLOCK), f32),
            jax.ShapeDtypeStruct((SLOTS + 1, BLOCK, D), bf16),
            jax.ShapeDtypeStruct((NX, META, D), bf16),
            jax.ShapeDtypeStruct((SLOTS + 2,), i32),
            jax.ShapeDtypeStruct((SLOTS + 1,), f32),
        ),
        in_specs=[smem()] + [vmem()] * (NX + 1),
        out_specs=(vmem(),) * 3 + (smem(), smem()),
        scratch_shapes=[pltpu.VMEM((SLOTS, BLOCK, wide), f32)]
        + [pltpu.VMEM((8, wide), f32)] * 2,
        compiler_params=limit(16),
        name="totals",
    )(where, *pieces, every_query)
    stats = lax.all_to_all(stats, QROWS, 0, 0, tiled=True)
    item_parts, norms = pl.pallas_call(
        item_kernel,
        out_shape=(
            jax.ShapeDtypeStruct((NY * NX, SLOTS_DEV * PART + META, D), bf16),
            jax.ShapeDtypeStruct((1, wide), f32),
        ),
        in_specs=[smem()] * 3 + [vmem()] * 4,
        out_specs=(vmem(),) * 2,
        scratch_shapes=[pltpu.VMEM((2 * BLOCK, wide), bf16)],
        compiler_params=limit(12),
        name="items",
    )(where, live, shifts, rows_all, metas, every_query, stats)

    item_parts = lax.all_to_all(item_parts, ("y", "x"), 0, 0, tiled=True)
    query_parts = pl.pallas_call(
        query_kernel,
        out_shape=jax.ShapeDtypeStruct((NQ, D + META, BLOCK), bf16),
        in_specs=[smem(), smem()] + [vmem()] * 3,
        out_specs=vmem(),
        scratch_shapes=[pltpu.VMEM((D, wide), f32), pltpu.VMEM((8, wide), f32), pltpu.VMEM((1, wide), f32)],
        compiler_params=limit(8),
        cost_estimate=pl.CostEstimate(flops=1 << 31, bytes_accessed=6 << 20, transcendentals=0),
        name="query_parts",
    )(live, shifts, rows_all, every_query, norms)
    part = pl.pallas_call(
        gather_parts_kernel,
        out_shape=jax.ShapeDtypeStruct((BLOCKS_DEV, PART, D), bf16),
        in_specs=[vmem()],
        out_specs=vmem(),
        scratch_shapes=[pltpu.VMEM((BLOCKS_DEV, PART, D), f32)],
        compiler_params=limit(4),
        name="gather_parts",
    )(item_parts)
    halves = [part[: BLOCKS_DEV // 2], part[BLOCKS_DEV // 2 :]]
    inner, outer = [(0, 1), (1, 0), (2, 3), (3, 2)], [(1, 2), (2, 1), (3, 0), (0, 3)]
    others = []
    for n, turn in enumerate((inner, outer)):
        others.append(lax.ppermute(halves[n], "zh", turn))
    halves = [
        lax.optimization_barrier((mine.astype(f32) + other.astype(f32)).astype(bf16))
        for mine, other in zip(halves, others)
    ]
    others = []
    for n, turn in enumerate((outer, inner)):
        others.append(lax.ppermute(halves[n], "zh", turn))
    part = jnp.concatenate([mine.astype(f32) + other.astype(f32) for mine, other in zip(halves, others)])
    query_parts = lax.all_to_all(query_parts, QROWS, 0, 0, tiled=True)
    loss, query_grad = pl.pallas_call(
        query_sum_kernel,
        out_shape=(jax.ShapeDtypeStruct((1, BLOCK), f32), jax.ShapeDtypeStruct((1, BLOCK, D), f32)),
        in_specs=[smem(), vmem(), vmem()],
        out_specs=(vmem(), vmem()),
        compiler_params=limit(4),
        name="query_sum",
    )(where, norms, query_parts)
    grads = [part]
    for k in range(1, NY):
        grads.append(lax.ppermute(part, "y", [(i, (i + k) % NY) for i in range(NY)]))

    new_table, new_first, new_second = pl.pallas_call(
        adam_kernel,
        out_shape=(jax.ShapeDtypeStruct(table.shape, f32),) * 3,
        in_specs=[smem()] + [vmem()] * (NY + 3),
        out_specs=(hbm(),) * 3,
        scratch_shapes=[pltpu.VMEM(table.shape, f32)] * 3 + [pltpu.SemaphoreType.DMA((BLOCKS_DEV, 3))],
        compiler_params=limit(12),
        name="adam",
    )(where, *grads, table, first_moment, second_moment)
    return loss, query_grad, new_table, new_first, new_second


def solution(mesh):
    fine = Mesh(mesh.devices.reshape(4, NY, NX, NZ, NC), ("zh", "y", "x", "zl", "c"))
    rep = ("zh", "y")
    shard = ("x", "zl", "c")
    in_specs = (
        P(rep, shard, None),
        P(rep, shard),
        P(rep, shard),
        P(rep, shard),
        P(rep, shard),
        P(shard, None),
        P(shard, None),
        P(shard, None),
    )
    out_specs = (
        P(rep, shard),
        P(rep, shard, None),
        P(shard, None),
        P(shard, None),
        P(shard, None),
    )
    return jax.shard_map(step, mesh=fine, in_specs=in_specs, out_specs=out_specs, check_vma=False)
```

```python
import jax
import jax.numpy as jnp
from jax import lax
from jax.experimental import pallas as pl
from jax.experimental.pallas import tpu as pltpu
from jax.sharding import Mesh, PartitionSpec as P


BLOCK = 128
D = 256
SLOTS_DEV = 4
BLOCKS_DEV = 6
NX = 4
NY = 4
NZ = 4
NC = 2
NQ = NZ * NC
SLOTS = NX * SLOTS_DEV
PART = BLOCK // NY
META = 8
CHUNK = 256
CHUNKS = NQ * BLOCK // CHUNK
TOGETHER = 4
QROWS = ("c", "zl")

logit_scale = 2.0
beta_first = 0.9
beta_second = 0.99
learn_rate = 0.01
adam_eps = 1e-08
bias_first = 1.0 - 0.9**10
bias_second = 1.0 - 0.99**10
floor_value = -1e30

f32 = jnp.float32
bf16 = jnp.bfloat16
i32 = jnp.int32


def vmem():
    return pl.BlockSpec(memory_space=pltpu.VMEM)


def hbm():
    return pl.BlockSpec(memory_space=pltpu.HBM)


def smem():
    return pl.BlockSpec(memory_space=pltpu.SMEM)


def limit(mib):
    return pltpu.CompilerParams(vmem_limit_bytes=mib << 20)


def pack_kernel(ids, count, logq, table, queries, targets, item_out, query_out):
    slot = (targets[...] >> 7).astype(f32)
    item = (targets[...] & (BLOCK - 1)).astype(f32)
    both = jnp.broadcast_to(jnp.concatenate([slot, item], axis=1), (META, D)).astype(bf16)
    for z in range(NZ):
        query_out[z, pl.ds(0, BLOCK), :] = queries[0]
        query_out[z, pl.ds(BLOCK, META), :] = both
    row = lax.broadcasted_iota(i32, (META, D), 0)
    lane = lax.broadcasted_iota(i32, (META, D), 1)
    meta = jnp.where(row == 4, count[0, 0].astype(f32), 0.0)
    for j in range(SLOTS_DEV):
        whole = jnp.full((META, D), logq[0, j], f32)
        high = whole.astype(bf16).astype(f32)
        mid = (whole - high).astype(bf16).astype(f32)
        low = whole - high - mid
        ident = jnp.full((META, D), ids[0, j].astype(f32), f32)
        value = jnp.where(row == 0, high, jnp.where(row == 1, mid, jnp.where(row == 2, low, ident)))
        meta = jnp.where((lane == j) & (row < 4), value, meta)
    item_out[pl.ds(SLOTS_DEV * BLOCK, META), :] = meta.astype(bf16)
    for j in range(SLOTS_DEV):
        rows = table[pl.ds(pl.multiple_of(ids[0, j] * BLOCK, BLOCK), BLOCK), :]
        item_out[pl.ds(j * BLOCK, BLOCK), :] = (logit_scale * rows.astype(bf16).astype(f32)).astype(bf16)


def query_chunk(queries, b):
    return jnp.concatenate([queries[2 * b, pl.ds(0, BLOCK), :], queries[2 * b + 1, pl.ds(0, BLOCK), :]], axis=0)


def target_codes(queries):
    parts = []
    for r in range(NQ):
        row = queries[r, pl.ds(BLOCK, META), :].astype(f32)[0:1]
        parts.append((row[:, :BLOCK] * BLOCK + row[:, BLOCK:]).astype(i32))
    return jnp.concatenate(parts, axis=1)


def totals_kernel(
    place, own, one, two, three, queries,
    out, rows_all, metas, live, shifts, scores, tops, sums,
):
    lane = lax.broadcasted_iota(i32, (1, D), 1)
    number = jnp.int32(0)
    for k, piece in enumerate((own, one, two, three)):
        x = (place[2] - k) & (NX - 1)
        raw = piece[pl.ds(SLOTS_DEV * BLOCK, META), :]
        metas[x] = raw
        meta = raw.astype(f32)
        row = meta[0:1] + meta[1:2] + meta[2:3]
        count = jnp.max(meta[4:5]).astype(i32)
        for j in range(SLOTS_DEV):
            shifts[number] = jnp.sum(jnp.where(lane == j, row, 0.0))
            live[number] = x * (NQ * SLOTS_DEV) + place[0] * SLOTS_DEV + j
            rows_all[number] = piece[pl.ds(j * BLOCK, BLOCK), :]
            number = number + (j < count).astype(i32)
    live[SLOTS + 1] = number

    def pad(i, carry):
        rows_all[i] = jnp.zeros((BLOCK, D), bf16)
        shifts[i] = -floor_value
        live[i] = -1
        return carry

    lax.fori_loop(number, (number + TOGETHER - 1) // TOGETHER * TOGETHER, pad, 0)
    pairs = (number + 1) // 2
    tops[...] = jnp.full(tops.shape, floor_value, f32)
    sums[...] = jnp.zeros(sums.shape, f32)

    def score(g, carry):
        rows = rows_all[pl.ds(g * TOGETHER, TOGETHER)].reshape(TOGETHER * BLOCK, D)
        for b in range(CHUNKS):
            cols = pl.ds(b * CHUNK, CHUNK)
            doubled = pair_products(rows, queries, b)
            top = tops[:, cols]
            for h in range(TOGETHER):
                i = g * TOGETHER + h
                block = doubled[h * BLOCK : (h + 1) * BLOCK]
                scores[i, :, cols] = block
                top = jnp.maximum(top, jnp.max(block.reshape(BLOCK // 8, 8, CHUNK), axis=0) - shifts[i])
            tops[:, cols] = top
        return carry

    lax.fori_loop(0, (number + TOGETHER - 1) // TOGETHER, score, 0)
    top_row = jnp.max(tops[...], axis=0, keepdims=True)

    def weigh(p, carry):
        for h in range(2):
            i = 2 * p + h
            for b in range(CHUNKS):
                cols = pl.ds(b * CHUNK, CHUNK)
                base = top_row[:, b * CHUNK : (b + 1) * CHUNK] + shifts[i]
                weight = jnp.exp(scores[i, :, cols] - base)
                sums[:, cols] = sums[:, cols] + jnp.sum(weight.reshape(BLOCK // 8, 8, CHUNK), axis=0)
        return carry

    lax.fori_loop(0, pairs, weigh, 0)
    norm = top_row + jnp.log(jnp.sum(sums[...], axis=0, keepdims=True))
    norms = jnp.concatenate([norm[:, r * BLOCK : (r + 1) * BLOCK] for r in range(NQ)], axis=0)
    for d in range(NQ):
        out[d] = norms


def pair_products(rows, queries, b):
    return lax.dot_general(rows, query_chunk(queries, b), (((1,), (1,)), ((), ())), preferred_element_type=f32)


def dlogits(doubled, norm, codes, live, shifts, i):
    probs = jnp.exp(doubled - (norm + shifts[i]))
    item_index = lax.broadcasted_iota(i32, (BLOCK, CHUNK), 0)
    return jnp.where(item_index == codes - live[i] * BLOCK, probs - 1.0, probs).astype(bf16)


def item_kernel(place, live, shifts, rows_all, metas, queries, stats, item_out, norm_out, held):
    top = stats[0]
    for r in range(1, NQ):
        top = jnp.maximum(top, stats[r])
    total = jnp.zeros_like(top)
    for r in range(NQ):
        total = total + jnp.exp(stats[r] - top)
    norms = top + jnp.log(total)
    norm_row = jnp.concatenate([norms[r : r + 1] for r in range(NQ)], axis=1)
    norm_out[...] = norm_row
    codes = target_codes(queries)
    item_out[...] = jnp.zeros(item_out.shape, bf16)
    for x in range(NX):
        for y in range(NY):
            item_out[y * NX + x, pl.ds(SLOTS_DEV * PART, META), :] = metas[x]
    number = live[SLOTS + 1]

    def one_pair(p, carry):
        rows = rows_all[pl.ds(2 * p, 2)].reshape(2 * BLOCK, D)
        for b in range(CHUNKS):
            doubled = pair_products(rows, queries, b)
            norm = norm_row[:, b * CHUNK : (b + 1) * CHUNK]
            code = codes[:, b * CHUNK : (b + 1) * CHUNK]
            for h in range(2):
                half = pl.ds(h * BLOCK, BLOCK)
                held[half, pl.ds(b * CHUNK, CHUNK)] = dlogits(
                    doubled[h * BLOCK : (h + 1) * BLOCK], norm, code, live, shifts, 2 * p + h
                )
        every = jnp.concatenate([query_chunk(queries, b) for b in range(CHUNKS)], axis=0)
        total = jnp.dot(held[...], every, preferred_element_type=f32)
        for h in range(2):
            i = 2 * p + h
            part = (logit_scale * total[h * BLOCK : (h + 1) * BLOCK]).astype(bf16)

            @pl.when(i < number)
            def _():
                x = live[i] // (NQ * SLOTS_DEV)
                rows = pl.ds(pl.multiple_of(live[i] % SLOTS_DEV * PART, PART), PART)
                for y in range(NY):
                    item_out[y * NX + x, rows, :] = part[y * PART : (y + 1) * PART]

        return carry

    lax.fori_loop(0, (number + 1) // 2, one_pair, 0)


def query_kernel(live, shifts, rows_all, queries, norms, out, total, picks, taken):
    codes = target_codes(queries)
    norm_row = norms[...]
    total[...] = jnp.zeros(total.shape, f32)
    picks[...] = jnp.zeros(picks.shape, f32)
    taken[...] = jnp.zeros(taken.shape, f32)
    item_index = lax.broadcasted_iota(i32, (BLOCK, CHUNK), 0)

    def one_group(g, carry):
        rows = rows_all[pl.ds(g * TOGETHER, TOGETHER)].reshape(TOGETHER * BLOCK, D)
        turned = rows.T
        for b in range(CHUNKS):
            cols = pl.ds(b * CHUNK, CHUNK)
            doubled = pair_products(rows, queries, b)
            norm = norm_row[:, b * CHUNK : (b + 1) * CHUNK]
            code = codes[:, b * CHUNK : (b + 1) * CHUNK]
            parts = []
            for h in range(TOGETHER):
                i = g * TOGETHER + h
                block = doubled[h * BLOCK : (h + 1) * BLOCK]
                wanted = code - live[i] * BLOCK
                match = item_index == wanted
                marked = jnp.where(match, block, 0.0)
                picks[:, cols] = picks[:, cols] + jnp.sum(marked.reshape(BLOCK // 8, 8, CHUNK), axis=0)
                here = (wanted >= 0) & (wanted < BLOCK)
                taken[:, cols] = taken[:, cols] + jnp.where(here, shifts[i], 0.0)
                probs = jnp.exp(block - (norm + shifts[i]))
                parts.append(jnp.where(match, probs - 1.0, probs).astype(bf16))
            total[:, cols] = total[:, cols] + jnp.dot(
                turned, jnp.concatenate(parts, axis=0), preferred_element_type=f32
            )
        return carry

    lax.fori_loop(0, (live[SLOTS + 1] + TOGETHER - 1) // TOGETHER, one_group, 0)
    row = lax.broadcasted_iota(i32, (META, BLOCK), 0)
    for r in range(NQ):
        cols = pl.ds(r * BLOCK, BLOCK)
        out[r, pl.ds(0, D), :] = total[:, cols].astype(bf16)
        pick = jnp.sum(picks[:, cols], axis=0, keepdims=True) - taken[:, cols]
        pick = jnp.broadcast_to(pick, (META, BLOCK))
        high = pick.astype(bf16).astype(f32)
        mid = (pick - high).astype(bf16).astype(f32)
        low = pick - high - mid
        three = jnp.where(row == 0, high, jnp.where(row == 1, mid, jnp.where(row == 2, low, 0.0)))
        out[r, pl.ds(D, META), :] = three.astype(bf16)


def gather_parts_kernel(parts, out, total):
    lane = lax.broadcasted_iota(i32, (1, D), 1)
    total[...] = jnp.zeros(total.shape, f32)
    for y in range(NY):
        meta = parts[y * NX, pl.ds(SLOTS_DEV * PART, META), :].astype(f32)
        for j in range(SLOTS_DEV):
            block = jnp.sum(jnp.where(lane == j, meta[3:4], 0.0)).astype(i32)
            piece = jnp.zeros((PART, D), f32)
            for x in range(NX):
                piece = piece + parts[y * NX + x, pl.ds(j * PART, PART), :].astype(f32)
            total[block] = total[block] + piece
    out[...] = total[...].astype(bf16)


def adam_kernel(place, own, one, two, three, table, first, second, *rest):
    outs, results, sems = rest[:3], rest[3:6], rest[6]
    copies = []
    for b in range(BLOCKS_DEV):
        for k, piece in enumerate((own, one, two, three)):
            y = (place[3] - k) & (NY - 1)
            rows = pl.ds(pl.multiple_of(b * BLOCK + y * PART, PART), PART)
            grad = piece[b]
            first_new = beta_first * first[rows, :] + (1.0 - beta_first) * grad
            second_new = beta_second * second[rows, :] + (1.0 - beta_second) * grad * grad
            results[1][rows, :] = first_new
            results[2][rows, :] = second_new
            results[0][rows, :] = table[rows, :] - learn_rate * (first_new / bias_first) / (
                jnp.sqrt(second_new / bias_second) + adam_eps
            )
        block = pl.ds(b * BLOCK, BLOCK)
        for n in range(3):
            copy = pltpu.make_async_copy(results[n].at[block, :], outs[n].at[block, :], sems.at[b, n])
            copy.start()
            copies.append(copy)
    for copy in copies:
        copy.wait()


def query_sum_kernel(place, norms, parts, loss_out, out):
    total = parts[0].astype(f32)
    for r in range(1, NQ):
        total = total + parts[r].astype(f32)
    out[0] = total[:D].T
    pick = jnp.sum(total[D : D + META], axis=0, keepdims=True)
    loss_out[...] = norms[:, pl.ds(pl.multiple_of(place[1] * BLOCK, BLOCK), BLOCK)] - pick


def step(queries, targets, samp_ids, counts, logq, table, first_moment, second_moment):
    place = lax.axis_index("zl") * NC + lax.axis_index("c")
    own = lax.axis_index("c") * NZ + lax.axis_index("zl")
    where = jnp.stack([place, own, lax.axis_index("x"), lax.axis_index("y")]).astype(i32)
    item_shape = jax.ShapeDtypeStruct((SLOTS_DEV * BLOCK + META, D), bf16)
    items, query_rows = pl.pallas_call(
        pack_kernel,
        out_shape=(item_shape, jax.ShapeDtypeStruct((NZ, BLOCK + META, D), bf16)),
        in_specs=[smem(), smem(), smem(), vmem(), vmem(), vmem()],
        out_specs=(vmem(), vmem()),
        name="pack",
    )(samp_ids, counts, logq, table, queries, targets)

    every_query = lax.all_to_all(query_rows, "zl", 0, 0, tiled=True)
    pieces = [items]
    for k in range(1, NX):
        pieces.append(lax.ppermute(items, "x", [(i, (i + k) % NX) for i in range(NX)]))
    every_query = lax.all_gather(every_query, "c", axis=0, tiled=True)

    wide = NQ * BLOCK
    stats, rows_all, metas, live, shifts = pl.pallas_call(
        totals_kernel,
        out_shape=(
            jax.ShapeDtypeStruct((NQ, NQ, BLOCK), f32),
            jax.ShapeDtypeStruct((SLOTS + 1, BLOCK, D), bf16),
            jax.ShapeDtypeStruct((NX, META, D), bf16),
            jax.ShapeDtypeStruct((SLOTS + 2,), i32),
            jax.ShapeDtypeStruct((SLOTS + 1,), f32),
        ),
        in_specs=[smem()] + [vmem()] * (NX + 1),
        out_specs=(vmem(),) * 3 + (smem(), smem()),
        scratch_shapes=[pltpu.VMEM((SLOTS, BLOCK, wide), f32)]
        + [pltpu.VMEM((8, wide), f32)] * 2,
        compiler_params=limit(16),
        name="totals",
    )(where, *pieces, every_query)
    stats = lax.all_to_all(stats, QROWS, 0, 0, tiled=True)
    item_parts, norms = pl.pallas_call(
        item_kernel,
        out_shape=(
            jax.ShapeDtypeStruct((NY * NX, SLOTS_DEV * PART + META, D), bf16),
            jax.ShapeDtypeStruct((1, wide), f32),
        ),
        in_specs=[smem()] * 3 + [vmem()] * 4,
        out_specs=(vmem(),) * 2,
        scratch_shapes=[pltpu.VMEM((2 * BLOCK, wide), bf16)],
        compiler_params=limit(12),
        name="items",
    )(where, live, shifts, rows_all, metas, every_query, stats)

    item_parts = lax.all_to_all(item_parts, ("y", "x"), 0, 0, tiled=True)
    query_parts = pl.pallas_call(
        query_kernel,
        out_shape=jax.ShapeDtypeStruct((NQ, D + META, BLOCK), bf16),
        in_specs=[smem(), smem()] + [vmem()] * 3,
        out_specs=vmem(),
        scratch_shapes=[pltpu.VMEM((D, wide), f32), pltpu.VMEM((8, wide), f32), pltpu.VMEM((1, wide), f32)],
        compiler_params=limit(8),
        cost_estimate=pl.CostEstimate(flops=1 << 31, bytes_accessed=6 << 20, transcendentals=0),
        name="query_parts",
    )(live, shifts, rows_all, every_query, norms)
    part = pl.pallas_call(
        gather_parts_kernel,
        out_shape=jax.ShapeDtypeStruct((BLOCKS_DEV, PART, D), bf16),
        in_specs=[vmem()],
        out_specs=vmem(),
        scratch_shapes=[pltpu.VMEM((BLOCKS_DEV, PART, D), f32)],
        compiler_params=limit(4),
        name="gather_parts",
    )(item_parts)
    other = lax.ppermute(part, "zh", [(0, 1), (1, 0), (2, 3), (3, 2)])
    part = lax.optimization_barrier((part.astype(f32) + other.astype(f32)).astype(bf16))
    other = lax.ppermute(part, "zh", [(1, 2), (2, 1), (3, 0), (0, 3)])
    part = part.astype(f32) + other.astype(f32)
    query_parts = lax.all_to_all(query_parts, QROWS, 0, 0, tiled=True)
    loss, query_grad = pl.pallas_call(
        query_sum_kernel,
        out_shape=(jax.ShapeDtypeStruct((1, BLOCK), f32), jax.ShapeDtypeStruct((1, BLOCK, D), f32)),
        in_specs=[smem(), vmem(), vmem()],
        out_specs=(vmem(), vmem()),
        compiler_params=limit(4),
        name="query_sum",
    )(where, norms, query_parts)
    grads = [part]
    for k in range(1, NY):
        grads.append(lax.ppermute(part, "y", [(i, (i + k) % NY) for i in range(NY)]))

    new_table, new_first, new_second = pl.pallas_call(
        adam_kernel,
        out_shape=(jax.ShapeDtypeStruct(table.shape, f32),) * 3,
        in_specs=[smem()] + [vmem()] * (NY + 3),
        out_specs=(hbm(),) * 3,
        scratch_shapes=[pltpu.VMEM(table.shape, f32)] * 3 + [pltpu.SemaphoreType.DMA((BLOCKS_DEV, 3))],
        compiler_params=limit(12),
        name="adam",
    )(where, *grads, table, first_moment, second_moment)
    return loss, query_grad, new_table, new_first, new_second


def solution(mesh):
    fine = Mesh(mesh.devices.reshape(4, NY, NX, NZ, NC), ("zh", "y", "x", "zl", "c"))
    rep = ("zh", "y")
    shard = ("x", "zl", "c")
    in_specs = (
        P(rep, shard, None),
        P(rep, shard),
        P(rep, shard),
        P(rep, shard),
        P(rep, shard),
        P(shard, None),
        P(shard, None),
        P(shard, None),
    )
    out_specs = (
        P(rep, shard),
        P(rep, shard, None),
        P(shard, None),
        P(shard, None),
        P(shard, None),
    )
    return jax.shard_map(step, mesh=fine, in_specs=in_specs, out_specs=out_specs, check_vma=False)
```

```python
import jax
import jax.numpy as jnp
from jax import lax
from jax.experimental import pallas as pl
from jax.experimental.pallas import tpu as pltpu
from jax.sharding import Mesh, PartitionSpec as P


BLOCK = 128
D = 256
SLOTS_DEV = 4
BLOCKS_DEV = 6
NX = 4
NY = 4
NZ = 4
NC = 2
NQ = NZ * NC
SLOTS = NX * SLOTS_DEV
PART = BLOCK // NY
META = 8
CHUNK = 256
CHUNKS = NQ * BLOCK // CHUNK
TOGETHER = 4
QROWS = ("c", "zl")

logit_scale = 2.0
beta_first = 0.9
beta_second = 0.99
learn_rate = 0.01
adam_eps = 1e-08
bias_first = 1.0 - 0.9**10
bias_second = 1.0 - 0.99**10
floor_value = -1e30

f32 = jnp.float32
bf16 = jnp.bfloat16
i32 = jnp.int32


def vmem():
    return pl.BlockSpec(memory_space=pltpu.VMEM)


def hbm():
    return pl.BlockSpec(memory_space=pltpu.HBM)


def smem():
    return pl.BlockSpec(memory_space=pltpu.SMEM)


def limit(mib):
    return pltpu.CompilerParams(vmem_limit_bytes=mib << 20)


def pack_kernel(ids, count, logq, table, queries, targets, item_out, query_out):
    slot = (targets[...] >> 7).astype(f32)
    item = (targets[...] & (BLOCK - 1)).astype(f32)
    both = jnp.broadcast_to(jnp.concatenate([slot, item], axis=1), (META, D)).astype(bf16)
    for z in range(NZ):
        query_out[z, pl.ds(0, BLOCK), :] = queries[0]
        query_out[z, pl.ds(BLOCK, META), :] = both
    row = lax.broadcasted_iota(i32, (META, D), 0)
    lane = lax.broadcasted_iota(i32, (META, D), 1)
    meta = jnp.where(row == 4, count[0, 0].astype(f32), 0.0)
    for j in range(SLOTS_DEV):
        whole = jnp.full((META, D), logq[0, j], f32)
        high = whole.astype(bf16).astype(f32)
        mid = (whole - high).astype(bf16).astype(f32)
        low = whole - high - mid
        ident = jnp.full((META, D), ids[0, j].astype(f32), f32)
        value = jnp.where(row == 0, high, jnp.where(row == 1, mid, jnp.where(row == 2, low, ident)))
        meta = jnp.where((lane == j) & (row < 4), value, meta)
    item_out[pl.ds(SLOTS_DEV * BLOCK, META), :] = meta.astype(bf16)
    for j in range(SLOTS_DEV):
        rows = table[pl.ds(pl.multiple_of(ids[0, j] * BLOCK, BLOCK), BLOCK), :]
        item_out[pl.ds(j * BLOCK, BLOCK), :] = (logit_scale * rows.astype(bf16).astype(f32)).astype(bf16)


def query_chunk(queries, b):
    return jnp.concatenate([queries[2 * b, pl.ds(0, BLOCK), :], queries[2 * b + 1, pl.ds(0, BLOCK), :]], axis=0)


def target_codes(queries):
    parts = []
    for r in range(NQ):
        row = queries[r, pl.ds(BLOCK, META), :].astype(f32)[0:1]
        parts.append((row[:, :BLOCK] * BLOCK + row[:, BLOCK:]).astype(i32))
    return jnp.concatenate(parts, axis=1)


def totals_kernel(
    place, own, one, two, three, queries,
    out, rows_all, metas, live, shifts, scores, tops, sums,
):
    lane = lax.broadcasted_iota(i32, (1, D), 1)
    number = jnp.int32(0)
    for k, piece in enumerate((own, one, two, three)):
        x = (place[2] - k) & (NX - 1)
        raw = piece[pl.ds(SLOTS_DEV * BLOCK, META), :]
        metas[x] = raw
        meta = raw.astype(f32)
        row = meta[0:1] + meta[1:2] + meta[2:3]
        count = jnp.max(meta[4:5]).astype(i32)
        for j in range(SLOTS_DEV):
            shifts[number] = jnp.sum(jnp.where(lane == j, row, 0.0))
            live[number] = x * (NQ * SLOTS_DEV) + place[0] * SLOTS_DEV + j
            rows_all[number] = piece[pl.ds(j * BLOCK, BLOCK), :]
            number = number + (j < count).astype(i32)
    live[SLOTS + 1] = number

    def pad(i, carry):
        rows_all[i] = jnp.zeros((BLOCK, D), bf16)
        shifts[i] = -floor_value
        live[i] = -1
        return carry

    lax.fori_loop(number, (number + TOGETHER - 1) // TOGETHER * TOGETHER, pad, 0)
    pairs = (number + 1) // 2
    tops[...] = jnp.full(tops.shape, floor_value, f32)
    sums[...] = jnp.zeros(sums.shape, f32)

    def score(g, carry):
        rows = rows_all[pl.ds(g * TOGETHER, TOGETHER)].reshape(TOGETHER * BLOCK, D)
        for b in range(CHUNKS):
            cols = pl.ds(b * CHUNK, CHUNK)
            doubled = pair_products(rows, queries, b)
            top = tops[:, cols]
            for h in range(TOGETHER):
                i = g * TOGETHER + h
                block = doubled[h * BLOCK : (h + 1) * BLOCK]
                scores[i, :, cols] = block
                top = jnp.maximum(top, jnp.max(block.reshape(BLOCK // 8, 8, CHUNK), axis=0) - shifts[i])
            tops[:, cols] = top
        return carry

    lax.fori_loop(0, (number + TOGETHER - 1) // TOGETHER, score, 0)
    top_row = jnp.max(tops[...], axis=0, keepdims=True)

    def weigh(p, carry):
        for h in range(2):
            i = 2 * p + h
            for b in range(CHUNKS):
                cols = pl.ds(b * CHUNK, CHUNK)
                base = top_row[:, b * CHUNK : (b + 1) * CHUNK] + shifts[i]
                weight = jnp.exp(scores[i, :, cols] - base)
                sums[:, cols] = sums[:, cols] + jnp.sum(weight.reshape(BLOCK // 8, 8, CHUNK), axis=0)
        return carry

    lax.fori_loop(0, pairs, weigh, 0)
    norm = top_row + jnp.log(jnp.sum(sums[...], axis=0, keepdims=True))
    norms = jnp.concatenate([norm[:, r * BLOCK : (r + 1) * BLOCK] for r in range(NQ)], axis=0)
    for d in range(NQ):
        out[d] = norms


def pair_products(rows, queries, b):
    return lax.dot_general(rows, query_chunk(queries, b), (((1,), (1,)), ((), ())), preferred_element_type=f32)


def dlogits(doubled, norm, codes, live, shifts, i):
    probs = jnp.exp(doubled - (norm + shifts[i]))
    item_index = lax.broadcasted_iota(i32, (BLOCK, CHUNK), 0)
    return jnp.where(item_index == codes - live[i] * BLOCK, probs - 1.0, probs).astype(bf16)


def item_kernel(place, live, shifts, rows_all, metas, queries, stats, item_out, norm_out, held):
    top = stats[0]
    for r in range(1, NQ):
        top = jnp.maximum(top, stats[r])
    total = jnp.zeros_like(top)
    for r in range(NQ):
        total = total + jnp.exp(stats[r] - top)
    norms = top + jnp.log(total)
    norm_row = jnp.concatenate([norms[r : r + 1] for r in range(NQ)], axis=1)
    norm_out[...] = norm_row
    codes = target_codes(queries)
    item_out[...] = jnp.zeros(item_out.shape, bf16)
    for x in range(NX):
        for y in range(NY):
            item_out[y * NX + x, pl.ds(SLOTS_DEV * PART, META), :] = metas[x]
    number = live[SLOTS + 1]

    def one_pair(p, carry):
        rows = rows_all[pl.ds(2 * p, 2)].reshape(2 * BLOCK, D)
        for b in range(CHUNKS):
            doubled = pair_products(rows, queries, b)
            norm = norm_row[:, b * CHUNK : (b + 1) * CHUNK]
            code = codes[:, b * CHUNK : (b + 1) * CHUNK]
            for h in range(2):
                half = pl.ds(h * BLOCK, BLOCK)
                held[half, pl.ds(b * CHUNK, CHUNK)] = dlogits(
                    doubled[h * BLOCK : (h + 1) * BLOCK], norm, code, live, shifts, 2 * p + h
                )
        every = jnp.concatenate([query_chunk(queries, b) for b in range(CHUNKS)], axis=0)
        total = jnp.dot(held[...], every, preferred_element_type=f32)
        for h in range(2):
            i = 2 * p + h
            part = (logit_scale * total[h * BLOCK : (h + 1) * BLOCK]).astype(bf16)

            @pl.when(i < number)
            def _():
                x = live[i] // (NQ * SLOTS_DEV)
                rows = pl.ds(pl.multiple_of(live[i] % SLOTS_DEV * PART, PART), PART)
                for y in range(NY):
                    item_out[y * NX + x, rows, :] = part[y * PART : (y + 1) * PART]

        return carry

    lax.fori_loop(0, (number + 1) // 2, one_pair, 0)


def query_kernel(live, shifts, rows_all, queries, norms, out, total, picks, taken):
    codes = target_codes(queries)
    norm_row = norms[...]
    total[...] = jnp.zeros(total.shape, f32)
    picks[...] = jnp.zeros(picks.shape, f32)
    taken[...] = jnp.zeros(taken.shape, f32)
    item_index = lax.broadcasted_iota(i32, (BLOCK, CHUNK), 0)

    def one_group(g, carry):
        rows = rows_all[pl.ds(g * TOGETHER, TOGETHER)].reshape(TOGETHER * BLOCK, D)
        turned = rows.T
        for b in range(CHUNKS):
            cols = pl.ds(b * CHUNK, CHUNK)
            doubled = pair_products(rows, queries, b)
            norm = norm_row[:, b * CHUNK : (b + 1) * CHUNK]
            code = codes[:, b * CHUNK : (b + 1) * CHUNK]
            parts = []
            for h in range(TOGETHER):
                i = g * TOGETHER + h
                block = doubled[h * BLOCK : (h + 1) * BLOCK]
                wanted = code - live[i] * BLOCK
                match = item_index == wanted
                marked = jnp.where(match, block, 0.0)
                picks[:, cols] = picks[:, cols] + jnp.sum(marked.reshape(BLOCK // 8, 8, CHUNK), axis=0)
                here = (wanted >= 0) & (wanted < BLOCK)
                taken[:, cols] = taken[:, cols] + jnp.where(here, shifts[i], 0.0)
                probs = jnp.exp(block - (norm + shifts[i]))
                parts.append(jnp.where(match, probs - 1.0, probs).astype(bf16))
            total[:, cols] = total[:, cols] + jnp.dot(
                turned, jnp.concatenate(parts, axis=0), preferred_element_type=f32
            )
        return carry

    lax.fori_loop(0, (live[SLOTS + 1] + TOGETHER - 1) // TOGETHER, one_group, 0)
    row = lax.broadcasted_iota(i32, (META, BLOCK), 0)
    for r in range(NQ):
        cols = pl.ds(r * BLOCK, BLOCK)
        out[r, pl.ds(0, D), :] = total[:, cols].astype(bf16)
        pick = jnp.sum(picks[:, cols], axis=0, keepdims=True) - taken[:, cols]
        pick = jnp.broadcast_to(pick, (META, BLOCK))
        high = pick.astype(bf16).astype(f32)
        mid = (pick - high).astype(bf16).astype(f32)
        low = pick - high - mid
        three = jnp.where(row == 0, high, jnp.where(row == 1, mid, jnp.where(row == 2, low, 0.0)))
        out[r, pl.ds(D, META), :] = three.astype(bf16)


def gather_parts_kernel(parts, out, total):
    lane = lax.broadcasted_iota(i32, (1, D), 1)
    total[...] = jnp.zeros(total.shape, f32)
    for y in range(NY):
        meta = parts[y * NX, pl.ds(SLOTS_DEV * PART, META), :].astype(f32)
        for j in range(SLOTS_DEV):
            block = jnp.sum(jnp.where(lane == j, meta[3:4], 0.0)).astype(i32)
            piece = jnp.zeros((PART, D), f32)
            for x in range(NX):
                piece = piece + parts[y * NX + x, pl.ds(j * PART, PART), :].astype(f32)
            total[block] = total[block] + piece
    out[...] = total[...].astype(bf16)


def adam_kernel(place, own, one, two, three, table, first, second, *rest):
    outs, results, sems = rest[:3], rest[3:6], rest[6]
    copies = []
    for b in range(BLOCKS_DEV):
        for k, piece in enumerate((own, one, two, three)):
            y = (place[3] - k) & (NY - 1)
            rows = pl.ds(pl.multiple_of(b * BLOCK + y * PART, PART), PART)
            grad = piece[b]
            first_new = beta_first * first[rows, :] + (1.0 - beta_first) * grad
            second_new = beta_second * second[rows, :] + (1.0 - beta_second) * grad * grad
            results[1][rows, :] = first_new
            results[2][rows, :] = second_new
            results[0][rows, :] = table[rows, :] - learn_rate * (first_new / bias_first) / (
                jnp.sqrt(second_new / bias_second) + adam_eps
            )
        block = pl.ds(b * BLOCK, BLOCK)
        for n in range(3):
            copy = pltpu.make_async_copy(results[n].at[block, :], outs[n].at[block, :], sems.at[b, n])
            copy.start()
            copies.append(copy)
    for copy in copies:
        copy.wait()


def query_sum_kernel(place, norms, parts, loss_out, out):
    total = parts[0].astype(f32)
    for r in range(1, NQ):
        total = total + parts[r].astype(f32)
    out[0] = total[:D].T
    pick = jnp.sum(total[D : D + META], axis=0, keepdims=True)
    loss_out[...] = norms[:, pl.ds(pl.multiple_of(place[1] * BLOCK, BLOCK), BLOCK)] - pick


def step(queries, targets, samp_ids, counts, logq, table, first_moment, second_moment):
    place = lax.axis_index("zl") * NC + lax.axis_index("c")
    own = lax.axis_index("c") * NZ + lax.axis_index("zl")
    where = jnp.stack([place, own, lax.axis_index("x"), lax.axis_index("y")]).astype(i32)
    item_shape = jax.ShapeDtypeStruct((SLOTS_DEV * BLOCK + META, D), bf16)
    items, query_rows = pl.pallas_call(
        pack_kernel,
        out_shape=(item_shape, jax.ShapeDtypeStruct((NZ, BLOCK + META, D), bf16)),
        in_specs=[smem(), smem(), smem(), vmem(), vmem(), vmem()],
        out_specs=(vmem(), vmem()),
        name="pack",
    )(samp_ids, counts, logq, table, queries, targets)

    every_query = lax.all_to_all(query_rows, "zl", 0, 0, tiled=True)
    pieces = [items]
    for k in range(1, NX):
        pieces.append(lax.ppermute(items, "x", [(i, (i + k) % NX) for i in range(NX)]))
    every_query = lax.all_gather(every_query, "c", axis=0, tiled=True)

    wide = NQ * BLOCK
    stats, rows_all, metas, live, shifts = pl.pallas_call(
        totals_kernel,
        out_shape=(
            jax.ShapeDtypeStruct((NQ, NQ, BLOCK), f32),
            jax.ShapeDtypeStruct((SLOTS + 1, BLOCK, D), bf16),
            jax.ShapeDtypeStruct((NX, META, D), bf16),
            jax.ShapeDtypeStruct((SLOTS + 2,), i32),
            jax.ShapeDtypeStruct((SLOTS + 1,), f32),
        ),
        in_specs=[smem()] + [vmem()] * (NX + 1),
        out_specs=(vmem(),) * 3 + (smem(), smem()),
        scratch_shapes=[pltpu.VMEM((SLOTS, BLOCK, wide), f32)]
        + [pltpu.VMEM((8, wide), f32)] * 2,
        compiler_params=limit(16),
        name="totals",
    )(where, *pieces, every_query)
    stats = lax.all_to_all(stats, QROWS, 0, 0, tiled=True)
    item_parts, norms = pl.pallas_call(
        item_kernel,
        out_shape=(
            jax.ShapeDtypeStruct((NY * NX, SLOTS_DEV * PART + META, D), bf16),
            jax.ShapeDtypeStruct((1, wide), f32),
        ),
        in_specs=[smem()] * 3 + [vmem()] * 4,
        out_specs=(vmem(),) * 2,
        scratch_shapes=[pltpu.VMEM((2 * BLOCK, wide), bf16)],
        compiler_params=limit(12),
        name="items",
    )(where, live, shifts, rows_all, metas, every_query, stats)

    item_parts = lax.all_to_all(item_parts, ("y", "x"), 0, 0, tiled=True)
    query_parts = pl.pallas_call(
        query_kernel,
        out_shape=jax.ShapeDtypeStruct((NQ, D + META, BLOCK), bf16),
        in_specs=[smem(), smem()] + [vmem()] * 3,
        out_specs=vmem(),
        scratch_shapes=[pltpu.VMEM((D, wide), f32), pltpu.VMEM((8, wide), f32), pltpu.VMEM((1, wide), f32)],
        compiler_params=limit(8),
        cost_estimate=pl.CostEstimate(flops=1 << 31, bytes_accessed=6 << 20, transcendentals=0),
        name="query_parts",
    )(live, shifts, rows_all, every_query, norms)
    part = pl.pallas_call(
        gather_parts_kernel,
        out_shape=jax.ShapeDtypeStruct((BLOCKS_DEV, PART, D), bf16),
        in_specs=[vmem()],
        out_specs=vmem(),
        scratch_shapes=[pltpu.VMEM((BLOCKS_DEV, PART, D), f32)],
        compiler_params=limit(4),
        name="gather_parts",
    )(item_parts)
    inner, outer = (1, 0, 3, 2), (3, 2, 1, 0)
    first = [(z * NC + c, (inner, outer)[c][z] * NC + c) for z in range(4) for c in range(NC)]
    second = [(z * NC + c, (outer, inner)[c][z] * NC + c) for z in range(4) for c in range(NC)]
    other = lax.ppermute(part, ("zh", "c"), first)
    part = lax.optimization_barrier((part.astype(f32) + other.astype(f32)).astype(bf16))
    other = lax.ppermute(part, ("zh", "c"), second)
    part = part.astype(f32) + other.astype(f32)
    query_parts = lax.all_to_all(query_parts, QROWS, 0, 0, tiled=True)
    loss, query_grad = pl.pallas_call(
        query_sum_kernel,
        out_shape=(jax.ShapeDtypeStruct((1, BLOCK), f32), jax.ShapeDtypeStruct((1, BLOCK, D), f32)),
        in_specs=[smem(), vmem(), vmem()],
        out_specs=(vmem(), vmem()),
        compiler_params=limit(4),
        name="query_sum",
    )(where, norms, query_parts)
    grads = [part]
    for k in range(1, NY):
        grads.append(lax.ppermute(part, "y", [(i, (i + k) % NY) for i in range(NY)]))

    new_table, new_first, new_second = pl.pallas_call(
        adam_kernel,
        out_shape=(jax.ShapeDtypeStruct(table.shape, f32),) * 3,
        in_specs=[smem()] + [vmem()] * (NY + 3),
        out_specs=(hbm(),) * 3,
        scratch_shapes=[pltpu.VMEM(table.shape, f32)] * 3 + [pltpu.SemaphoreType.DMA((BLOCKS_DEV, 3))],
        compiler_params=limit(12),
        name="adam",
    )(where, *grads, table, first_moment, second_moment)
    return loss, query_grad, new_table, new_first, new_second


def solution(mesh):
    fine = Mesh(mesh.devices.reshape(4, NY, NX, NZ, NC), ("zh", "y", "x", "zl", "c"))
    rep = ("zh", "y")
    shard = ("x", "zl", "c")
    in_specs = (
        P(rep, shard, None),
        P(rep, shard),
        P(rep, shard),
        P(rep, shard),
        P(rep, shard),
        P(shard, None),
        P(shard, None),
        P(shard, None),
    )
    out_specs = (
        P(rep, shard),
        P(rep, shard, None),
        P(shard, None),
        P(shard, None),
        P(shard, None),
    )
    return jax.shard_map(step, mesh=fine, in_specs=in_specs, out_specs=out_specs, check_vma=False)
```

```python
import functools

import jax
import jax.numpy as jnp
from jax import lax
from jax.experimental import pallas as pl
from jax.experimental.pallas import tpu as pltpu
from jax.sharding import Mesh, PartitionSpec as P


BLOCK = 128
D = 256
SLOTS_DEV = 4
BLOCKS_DEV = 6
NX = 4
NY = 4
NZ = 4
NC = 2
NQ = NZ * NC
SLOTS = NX * SLOTS_DEV
PART = BLOCK // NY
META = 8
CHUNK = 256
CHUNKS = NQ * BLOCK // CHUNK
TOGETHER = 4
QROWS = ("c", "zl")

logit_scale = 2.0
beta_first = 0.9
beta_second = 0.99
learn_rate = 0.01
adam_eps = 1e-08
bias_first = 1.0 - 0.9**10
bias_second = 1.0 - 0.99**10
floor_value = -1e30

f32 = jnp.float32
bf16 = jnp.bfloat16
i32 = jnp.int32


def vmem():
    return pl.BlockSpec(memory_space=pltpu.VMEM)


def hbm():
    return pl.BlockSpec(memory_space=pltpu.HBM)


def smem():
    return pl.BlockSpec(memory_space=pltpu.SMEM)


def limit(mib):
    return pltpu.CompilerParams(vmem_limit_bytes=mib << 20)


def pack_kernel(ids, count, logq, table, queries, targets, item_out, query_out):
    slot = (targets[...] >> 7).astype(f32)
    item = (targets[...] & (BLOCK - 1)).astype(f32)
    both = jnp.broadcast_to(jnp.concatenate([slot, item], axis=1), (META, D)).astype(bf16)
    for z in range(NZ):
        query_out[z, pl.ds(0, BLOCK), :] = queries[0]
        query_out[z, pl.ds(BLOCK, META), :] = both
    row = lax.broadcasted_iota(i32, (META, D), 0)
    lane = lax.broadcasted_iota(i32, (META, D), 1)
    meta = jnp.where(row == 4, count[0, 0].astype(f32), 0.0)
    for j in range(SLOTS_DEV):
        whole = jnp.full((META, D), logq[0, j], f32)
        high = whole.astype(bf16).astype(f32)
        mid = (whole - high).astype(bf16).astype(f32)
        low = whole - high - mid
        ident = jnp.full((META, D), ids[0, j].astype(f32), f32)
        value = jnp.where(row == 0, high, jnp.where(row == 1, mid, jnp.where(row == 2, low, ident)))
        meta = jnp.where((lane == j) & (row < 4), value, meta)
    item_out[pl.ds(SLOTS_DEV * BLOCK, META), :] = meta.astype(bf16)
    for j in range(SLOTS_DEV):
        rows = table[pl.ds(pl.multiple_of(ids[0, j] * BLOCK, BLOCK), BLOCK), :]
        item_out[pl.ds(j * BLOCK, BLOCK), :] = (logit_scale * rows.astype(bf16).astype(f32)).astype(bf16)


def query_chunk(queries, b):
    return jnp.concatenate([queries[2 * b, pl.ds(0, BLOCK), :], queries[2 * b + 1, pl.ds(0, BLOCK), :]], axis=0)


def target_codes(queries):
    parts = []
    for r in range(NQ):
        row = queries[r, pl.ds(BLOCK, META), :].astype(f32)[0:1]
        parts.append((row[:, :BLOCK] * BLOCK + row[:, BLOCK:]).astype(i32))
    return jnp.concatenate(parts, axis=1)


def totals_kernel(
    place, own, one, two, three, queries,
    out, rows_all, metas, live, shifts, scores, tops, sums,
):
    lane = lax.broadcasted_iota(i32, (1, D), 1)
    number = jnp.int32(0)
    for k, piece in enumerate((own, one, two, three)):
        x = (place[2] - k) & (NX - 1)
        raw = piece[pl.ds(SLOTS_DEV * BLOCK, META), :]
        metas[x] = raw
        meta = raw.astype(f32)
        row = meta[0:1] + meta[1:2] + meta[2:3]
        count = jnp.max(meta[4:5]).astype(i32)
        for j in range(SLOTS_DEV):
            shifts[number] = jnp.sum(jnp.where(lane == j, row, 0.0))
            live[number] = x * (NQ * SLOTS_DEV) + place[0] * SLOTS_DEV + j
            rows_all[number] = piece[pl.ds(j * BLOCK, BLOCK), :]
            number = number + (j < count).astype(i32)
    live[SLOTS + 1] = number

    def pad(i, carry):
        rows_all[i] = jnp.zeros((BLOCK, D), bf16)
        shifts[i] = -floor_value
        live[i] = -1
        return carry

    lax.fori_loop(number, (number + TOGETHER - 1) // TOGETHER * TOGETHER, pad, 0)
    pairs = (number + 1) // 2
    tops[...] = jnp.full(tops.shape, floor_value, f32)
    sums[...] = jnp.zeros(sums.shape, f32)

    def score(g, carry):
        rows = rows_all[pl.ds(g * TOGETHER, TOGETHER)].reshape(TOGETHER * BLOCK, D)
        for b in range(CHUNKS):
            cols = pl.ds(b * CHUNK, CHUNK)
            doubled = pair_products(rows, queries, b)
            top = tops[:, cols]
            for h in range(TOGETHER):
                i = g * TOGETHER + h
                block = doubled[h * BLOCK : (h + 1) * BLOCK]
                scores[i, :, cols] = block
                top = jnp.maximum(top, jnp.max(block.reshape(BLOCK // 8, 8, CHUNK), axis=0) - shifts[i])
            tops[:, cols] = top
        return carry

    lax.fori_loop(0, (number + TOGETHER - 1) // TOGETHER, score, 0)
    top_row = jnp.max(tops[...], axis=0, keepdims=True)

    def weigh(p, carry):
        for h in range(2):
            i = 2 * p + h
            for b in range(CHUNKS):
                cols = pl.ds(b * CHUNK, CHUNK)
                base = top_row[:, b * CHUNK : (b + 1) * CHUNK] + shifts[i]
                weight = jnp.exp(scores[i, :, cols] - base)
                sums[:, cols] = sums[:, cols] + jnp.sum(weight.reshape(BLOCK // 8, 8, CHUNK), axis=0)
        return carry

    lax.fori_loop(0, pairs, weigh, 0)
    norm = top_row + jnp.log(jnp.sum(sums[...], axis=0, keepdims=True))
    norms = jnp.concatenate([norm[:, r * BLOCK : (r + 1) * BLOCK] for r in range(NQ)], axis=0)
    for d in range(NQ):
        out[d] = norms


def pair_products(rows, queries, b):
    return lax.dot_general(rows, query_chunk(queries, b), (((1,), (1,)), ((), ())), preferred_element_type=f32)


def dlogits(doubled, norm, codes, live, shifts, i):
    probs = jnp.exp(doubled - (norm + shifts[i]))
    item_index = lax.broadcasted_iota(i32, (BLOCK, CHUNK), 0)
    return jnp.where(item_index == codes - live[i] * BLOCK, probs - 1.0, probs).astype(bf16)


def item_kernel(place, live, shifts, rows_all, metas, queries, stats, item_out, norm_out, held):
    top = stats[0]
    for r in range(1, NQ):
        top = jnp.maximum(top, stats[r])
    total = jnp.zeros_like(top)
    for r in range(NQ):
        total = total + jnp.exp(stats[r] - top)
    norms = top + jnp.log(total)
    norm_row = jnp.concatenate([norms[r : r + 1] for r in range(NQ)], axis=1)
    norm_out[...] = norm_row
    codes = target_codes(queries)
    item_out[...] = jnp.zeros(item_out.shape, bf16)
    for x in range(NX):
        for y in range(NY):
            item_out[y * NX + x, pl.ds(SLOTS_DEV * PART, META), :] = metas[x]
    number = live[SLOTS + 1]

    def one_pair(p, carry):
        rows = rows_all[pl.ds(2 * p, 2)].reshape(2 * BLOCK, D)
        for b in range(CHUNKS):
            doubled = pair_products(rows, queries, b)
            norm = norm_row[:, b * CHUNK : (b + 1) * CHUNK]
            code = codes[:, b * CHUNK : (b + 1) * CHUNK]
            for h in range(2):
                half = pl.ds(h * BLOCK, BLOCK)
                held[half, pl.ds(b * CHUNK, CHUNK)] = dlogits(
                    doubled[h * BLOCK : (h + 1) * BLOCK], norm, code, live, shifts, 2 * p + h
                )
        every = jnp.concatenate([query_chunk(queries, b) for b in range(CHUNKS)], axis=0)
        total = jnp.dot(held[...], every, preferred_element_type=f32)
        for h in range(2):
            i = 2 * p + h
            part = (logit_scale * total[h * BLOCK : (h + 1) * BLOCK]).astype(bf16)

            @pl.when(i < number)
            def _():
                x = live[i] // (NQ * SLOTS_DEV)
                rows = pl.ds(pl.multiple_of(live[i] % SLOTS_DEV * PART, PART), PART)
                for y in range(NY):
                    item_out[y * NX + x, rows, :] = part[y * PART : (y + 1) * PART]

        return carry

    lax.fori_loop(0, (number + 1) // 2, one_pair, 0)


def query_kernel(live, shifts, rows_all, queries, norms, out, total, picks, taken):
    codes = target_codes(queries)
    norm_row = norms[...]
    total[...] = jnp.zeros(total.shape, f32)
    picks[...] = jnp.zeros(picks.shape, f32)
    taken[...] = jnp.zeros(taken.shape, f32)
    item_index = lax.broadcasted_iota(i32, (BLOCK, CHUNK), 0)

    def one_group(g, carry):
        rows = rows_all[pl.ds(g * TOGETHER, TOGETHER)].reshape(TOGETHER * BLOCK, D)
        turned = rows.T
        for b in range(CHUNKS):
            cols = pl.ds(b * CHUNK, CHUNK)
            doubled = pair_products(rows, queries, b)
            norm = norm_row[:, b * CHUNK : (b + 1) * CHUNK]
            code = codes[:, b * CHUNK : (b + 1) * CHUNK]
            parts = []
            for h in range(TOGETHER):
                i = g * TOGETHER + h
                block = doubled[h * BLOCK : (h + 1) * BLOCK]
                wanted = code - live[i] * BLOCK
                match = item_index == wanted
                marked = jnp.where(match, block, 0.0)
                picks[:, cols] = picks[:, cols] + jnp.sum(marked.reshape(BLOCK // 8, 8, CHUNK), axis=0)
                here = (wanted >= 0) & (wanted < BLOCK)
                taken[:, cols] = taken[:, cols] + jnp.where(here, shifts[i], 0.0)
                probs = jnp.exp(block - (norm + shifts[i]))
                parts.append(jnp.where(match, probs - 1.0, probs).astype(bf16))
            total[:, cols] = total[:, cols] + jnp.dot(
                turned, jnp.concatenate(parts, axis=0), preferred_element_type=f32
            )
        return carry

    lax.fori_loop(0, (live[SLOTS + 1] + TOGETHER - 1) // TOGETHER, one_group, 0)
    row = lax.broadcasted_iota(i32, (META, BLOCK), 0)
    for r in range(NQ):
        cols = pl.ds(r * BLOCK, BLOCK)
        out[r, pl.ds(0, D), :] = total[:, cols].astype(bf16)
        pick = jnp.sum(picks[:, cols], axis=0, keepdims=True) - taken[:, cols]
        pick = jnp.broadcast_to(pick, (META, BLOCK))
        high = pick.astype(bf16).astype(f32)
        mid = (pick - high).astype(bf16).astype(f32)
        low = pick - high - mid
        three = jnp.where(row == 0, high, jnp.where(row == 1, mid, jnp.where(row == 2, low, 0.0)))
        out[r, pl.ds(D, META), :] = three.astype(bf16)


def gather_parts_kernel(parts, out, total):
    lane = lax.broadcasted_iota(i32, (1, D), 1)
    total[...] = jnp.zeros(total.shape, f32)
    for y in range(NY):
        meta = parts[y * NX, pl.ds(SLOTS_DEV * PART, META), :].astype(f32)
        for j in range(SLOTS_DEV):
            block = jnp.sum(jnp.where(lane == j, meta[3:4], 0.0)).astype(i32)
            piece = jnp.zeros((PART, D), f32)
            for x in range(NX):
                piece = piece + parts[y * NX + x, pl.ds(j * PART, PART), :].astype(f32)
            total[block] = total[block] + piece
    out[...] = total[...].astype(bf16)


def adam_kernel(steps, place, early, late, table, first, second, *rest):
    outs, results, sems = rest[-7:-4], rest[-4:-1], rest[-1]
    copies = []
    for b in range(BLOCKS_DEV):
        for n, piece in enumerate((early, late)):
            y = (place[3] - steps[n]) & (NY - 1)
            rows = pl.ds(pl.multiple_of(b * BLOCK + y * PART, PART), PART)
            grad = piece[b]
            first_new = beta_first * first[rows, :] + (1.0 - beta_first) * grad
            second_new = beta_second * second[rows, :] + (1.0 - beta_second) * grad * grad
            results[1][rows, :] = first_new
            results[2][rows, :] = second_new
            results[0][rows, :] = table[rows, :] - learn_rate * (first_new / bias_first) / (
                jnp.sqrt(second_new / bias_second) + adam_eps
            )
            for m in range(3):
                copy = pltpu.make_async_copy(results[m].at[rows, :], outs[m].at[rows, :], sems.at[b, n, m])
                copy.start()
                copies.append(copy)
    for copy in copies:
        copy.wait()


def query_sum_kernel(place, norms, parts, loss_out, out):
    total = parts[0].astype(f32)
    for r in range(1, NQ):
        total = total + parts[r].astype(f32)
    out[0] = total[:D].T
    pick = jnp.sum(total[D : D + META], axis=0, keepdims=True)
    loss_out[...] = norms[:, pl.ds(pl.multiple_of(place[1] * BLOCK, BLOCK), BLOCK)] - pick


def step(queries, targets, samp_ids, counts, logq, table, first_moment, second_moment):
    place = lax.axis_index("zl") * NC + lax.axis_index("c")
    own = lax.axis_index("c") * NZ + lax.axis_index("zl")
    where = jnp.stack([place, own, lax.axis_index("x"), lax.axis_index("y")]).astype(i32)
    item_shape = jax.ShapeDtypeStruct((SLOTS_DEV * BLOCK + META, D), bf16)
    items, query_rows = pl.pallas_call(
        pack_kernel,
        out_shape=(item_shape, jax.ShapeDtypeStruct((NZ, BLOCK + META, D), bf16)),
        in_specs=[smem(), smem(), smem(), vmem(), vmem(), vmem()],
        out_specs=(vmem(), vmem()),
        name="pack",
    )(samp_ids, counts, logq, table, queries, targets)

    every_query = lax.all_to_all(query_rows, "zl", 0, 0, tiled=True)
    pieces = [items]
    for k in range(1, NX):
        pieces.append(lax.ppermute(items, "x", [(i, (i + k) % NX) for i in range(NX)]))
    every_query = lax.all_gather(every_query, "c", axis=0, tiled=True)

    wide = NQ * BLOCK
    stats, rows_all, metas, live, shifts = pl.pallas_call(
        totals_kernel,
        out_shape=(
            jax.ShapeDtypeStruct((NQ, NQ, BLOCK), f32),
            jax.ShapeDtypeStruct((SLOTS + 1, BLOCK, D), bf16),
            jax.ShapeDtypeStruct((NX, META, D), bf16),
            jax.ShapeDtypeStruct((SLOTS + 2,), i32),
            jax.ShapeDtypeStruct((SLOTS + 1,), f32),
        ),
        in_specs=[smem()] + [vmem()] * (NX + 1),
        out_specs=(vmem(),) * 3 + (smem(), smem()),
        scratch_shapes=[pltpu.VMEM((SLOTS, BLOCK, wide), f32)]
        + [pltpu.VMEM((8, wide), f32)] * 2,
        compiler_params=limit(16),
        name="totals",
    )(where, *pieces, every_query)
    stats = lax.all_to_all(stats, QROWS, 0, 0, tiled=True)
    item_parts, norms = pl.pallas_call(
        item_kernel,
        out_shape=(
            jax.ShapeDtypeStruct((NY * NX, SLOTS_DEV * PART + META, D), bf16),
            jax.ShapeDtypeStruct((1, wide), f32),
        ),
        in_specs=[smem()] * 3 + [vmem()] * 4,
        out_specs=(vmem(),) * 2,
        scratch_shapes=[pltpu.VMEM((2 * BLOCK, wide), bf16)],
        compiler_params=limit(12),
        name="items",
    )(where, live, shifts, rows_all, metas, every_query, stats)

    item_parts = lax.all_to_all(item_parts, ("y", "x"), 0, 0, tiled=True)
    query_parts = pl.pallas_call(
        query_kernel,
        out_shape=jax.ShapeDtypeStruct((NQ, D + META, BLOCK), bf16),
        in_specs=[smem(), smem()] + [vmem()] * 3,
        out_specs=vmem(),
        scratch_shapes=[pltpu.VMEM((D, wide), f32), pltpu.VMEM((8, wide), f32), pltpu.VMEM((1, wide), f32)],
        compiler_params=limit(8),
        cost_estimate=pl.CostEstimate(flops=1 << 31, bytes_accessed=6 << 20, transcendentals=0),
        name="query_parts",
    )(live, shifts, rows_all, every_query, norms)
    part = pl.pallas_call(
        gather_parts_kernel,
        out_shape=jax.ShapeDtypeStruct((BLOCKS_DEV, PART, D), bf16),
        in_specs=[vmem()],
        out_specs=vmem(),
        scratch_shapes=[pltpu.VMEM((BLOCKS_DEV, PART, D), f32)],
        compiler_params=limit(4),
        name="gather_parts",
    )(item_parts)
    inner, outer = (1, 0, 3, 2), (3, 2, 1, 0)
    first = [(z * NC + c, (inner, outer)[c][z] * NC + c) for z in range(4) for c in range(NC)]
    second = [(z * NC + c, (outer, inner)[c][z] * NC + c) for z in range(4) for c in range(NC)]
    other = lax.ppermute(part, ("zh", "c"), first)
    part = lax.optimization_barrier((part.astype(f32) + other.astype(f32)).astype(bf16))
    other = lax.ppermute(part, ("zh", "c"), second)
    part = part.astype(f32) + other.astype(f32)
    query_parts = lax.all_to_all(query_parts, QROWS, 0, 0, tiled=True)
    loss, query_grad = pl.pallas_call(
        query_sum_kernel,
        out_shape=(jax.ShapeDtypeStruct((1, BLOCK), f32), jax.ShapeDtypeStruct((1, BLOCK, D), f32)),
        in_specs=[smem(), vmem(), vmem()],
        out_specs=(vmem(), vmem()),
        compiler_params=limit(4),
        name="query_sum",
    )(where, norms, query_parts)
    grads = [part]
    for k in range(1, NY):
        grads.append(lax.ppermute(part, "y", [(i, (i + k) % NY) for i in range(NY)]))

    def adam(steps, before):
        return pl.pallas_call(
            functools.partial(adam_kernel, steps),
            out_shape=(jax.ShapeDtypeStruct(table.shape, f32),) * 3,
            in_specs=[smem()] + [vmem()] * 5 + [hbm()] * len(before),
            out_specs=(hbm(),) * 3,
            scratch_shapes=[pltpu.VMEM(table.shape, f32)] * 3 + [pltpu.SemaphoreType.DMA((BLOCKS_DEV, 2, 3))],
            input_output_aliases={6 + n: n for n in range(len(before))},
            compiler_params=limit(12),
            cost_estimate=pl.CostEstimate(flops=1 << 22, bytes_accessed=3 << 20, transcendentals=0),
        )(where, grads[steps[0]], grads[steps[1]], table, first_moment, second_moment, *before)

    new = adam((0, 2), ())
    new_table, new_first, new_second = adam((1, 3), new)
    return loss, query_grad, new_table, new_first, new_second


def solution(mesh):
    fine = Mesh(mesh.devices.reshape(4, NY, NX, NZ, NC), ("zh", "y", "x", "zl", "c"))
    rep = ("zh", "y")
    shard = ("x", "zl", "c")
    in_specs = (
        P(rep, shard, None),
        P(rep, shard),
        P(rep, shard),
        P(rep, shard),
        P(rep, shard),
        P(shard, None),
        P(shard, None),
        P(shard, None),
    )
    out_specs = (
        P(rep, shard),
        P(rep, shard, None),
        P(shard, None),
        P(shard, None),
        P(shard, None),
    )
    return jax.shard_map(step, mesh=fine, in_specs=in_specs, out_specs=out_specs, check_vma=False)
```
